32 devices in a mesh: loan: 8 (over y, x, core), path: 4 (over z).
Axes of the slice: x: 2, y: 2, z: 4, core: 2. Of those that a mesh axis runs over, the one named last changes fastest.
Arguments:
- price_moves: bfloat16 [12, 416, 512], P(None, 'loan', 'path'), may hold values from -0.1796875 to 0.1796875
- block_regions: int32 [16, 32], P('loan'), may hold values from 0 to 415
- region_slot: int32 [4096], P('loan'), may hold values from 0 to 31
- block_pools: int32 [16, 32], P('loan'), may hold values from 0 to 511, as said below
- pool_slot: int32 [4096], P('loan'), may hold values from 0 to 31, as said below
- init_state: int32 [4096], P('loan'), may hold values from 0 to 5
- balance: float32 [4096], P('loan'), may hold values from 0.5 to 2
- loan_to_value: float32 [4096], P('loan'), may hold values from 0.5 to 1.3
- hazard_base: float32 [2, 6], replicated, may hold values from -4 to -1
- hazard_slope: float32 [2, 6], replicated, may hold values from 1 to 4
- attach_bps: int32 [512, 6], P('loan'), may hold values from 0 to 2995, as said below
Outputs:
- expected_loss: float32 [6, 3, 512], P(None, None, 'loan')
- path_loss: float32 [6, 512, 512], P(None, 'loan', 'path')
The draws below stay inside these ranges and needn't reach their ends.
Inputs may be any that keep to these rules, and one draw needn't show every extreme that they name: `block_pools`: over all blocks' lists every pool appears exactly once. The lists of the blocks held by one index of loan name exactly 64 // 8 pools of every owner, owner k being the index of loan that holds pools k * 64 to (k + 1) * 64 - 1. `pool_slot`: every aligned block of 256 loans uses each position of its pool list at least once. `attach_bps`: each row starts at 0 and rises by 100 to 599 from one tranche to the next.
All inputs are finite; a program needn't handle non-finite values.
Results may differ from the reference program's by a relative error of at most 0.0003.
Values may be sent and summed in bfloat16 or wider, within the bound.
No kernel may reach another device: no remote copies, remote signals or barrier semaphores. Data moves between devices by JAX's collectives and lax.ppermute only.
A program may use at most 64 MiB of HBM per device.

```python
import math
import jax
import jax.numpy as jnp
import numpy as np
from jax import lax

PATH_DEV = 128
BLOCK = 256
REG_BLOCK = 32
POOL_BLOCK = 32
METROS = 416
MONTHS = 12
LIVE = 6
TRANCHES = 6
DATES = 3
LOANS = 4096
BLOCKS = 16
POOL_DEV = 64
POOLS = 512
PATHS = 512
N_PATH = 4


def draw_block_pools(key, part):
    owners = POOLS // POOL_DEV
    per_owner = POOL_DEV // owners
    orders = jax.vmap(lambda o: jax.random.permutation(jax.random.fold_in(key, o), POOL_DEV))(jnp.arange(owners, dtype=jnp.int32))
    ranked = orders.reshape(owners, owners, per_owner).transpose(1, 0, 2) + (jnp.arange(owners, dtype=jnp.int32) * POOL_DEV)[None, :, None]
    device_rows = ranked.reshape(owners, POOL_DEV)
    shuffled = jax.vmap(lambda d, r: jax.random.permutation(jax.random.fold_in(key, 100003 + d), r))(jnp.arange(owners, dtype=jnp.int32), device_rows)
    return shuffled.reshape(BLOCKS, POOL_BLOCK).astype(jnp.int32)


def draw_pool_slot(key, part):

    def one_block(number):
        sub_key = jax.random.fold_in(key, number)
        filler = jax.random.randint(sub_key, (BLOCK - POOL_BLOCK,), 0, POOL_BLOCK, dtype=jnp.int32)
        whole = jnp.concatenate([jnp.arange(POOL_BLOCK, dtype=jnp.int32), filler])
        return jax.random.permutation(jax.random.fold_in(sub_key, 7), whole)
    return jax.vmap(one_block)(jnp.arange(BLOCKS, dtype=jnp.int32)).reshape(LOANS).astype(jnp.int32)


def draw_attach_bps(key, part):
    widths = jax.random.randint(key, (POOLS, TRANCHES - 1), 100, 600, dtype=jnp.int32)
    chosen = jax.random.randint(jax.random.fold_in(key, 31), (), 0, POOLS, dtype=jnp.int32)
    widest = jnp.arange(POOLS, dtype=jnp.int32)[:, None] == chosen
    widths = jnp.where(widest, jnp.int32(599), widths)
    starts = jnp.zeros((POOLS, 1), jnp.int32)
    return jnp.concatenate([starts, jnp.cumsum(widths, axis=1)], axis=1).astype(jnp.int32)


def set_ends(entries, rng, least, high):
    extent = entries.shape
    index_at = [jax.random.randint(jax.random.fold_in(rng, axis), (), 0, extent[axis]) for axis in range(len(extent))]
    entries = entries.at[tuple(index_at)].set(least)
    longest = extent.index(max(extent))
    index_at[longest] = (index_at[longest] + 1) % extent[longest]
    return entries.at[tuple(index_at)].set(high)


def level_of(rng, dims, split, low, high):
    gain = 1.0
    for axis_at, parts in split:
        steps = jax.random.uniform(jax.random.fold_in(jax.random.fold_in(rng, 6), axis_at), (parts,), jnp.float32, low / len(split), high / len(split))
        gain = gain * jnp.repeat(jnp.exp(steps), dims[axis_at] // parts).reshape((-1,) + (1,) * (len(dims) - 1 - axis_at))
    return gain


def rank_bounds(count, skew):
    portions = [(1 << 20) // math.isqrt(rank ** skew) + 1 for rank in range(1, count + 1)]
    width = 1 + sum(portions) // (1 << 30)
    return np.cumsum(np.array([max(1, weight // width) for weight in portions]))


def ranked_ids(rng, dims, amount, lean):
    table = rank_bounds(amount, lean)
    pick = jax.random.randint(jax.random.fold_in(rng, 1), dims, 0, int(table[amount - 1]))
    rank = jnp.searchsorted(jnp.asarray(table, jnp.int32), pick, side="right")
    return jax.random.permutation(jax.random.fold_in(rng, 2), amount)[rank].astype(jnp.int32)


def bell_draw(rng, dims, spread, reach, pieces=(), kind=jnp.bfloat16):
    result = spread * jax.random.normal(rng, dims, jnp.float32)
    if pieces:
        result = result * level_of(rng, dims, pieces, -0.22, 0.18)
    return jnp.clip(result, -reach, reach).astype(kind)


def setup_inputs(seed: int = 0) -> dict:
    keys = jax.random.split(jax.random.key(seed), 12)
    return {
        "price_moves": bell_draw(keys[0], (MONTHS, METROS, PATHS), 0.03, 0.1796875, ((1, 8), (2, 4))),
        "block_regions": set_ends(ranked_ids(keys[1], (BLOCKS, REG_BLOCK), METROS, 3), jax.random.fold_in(keys[1], 3), 0, METROS - 1).astype(jnp.int32),
        "region_slot": set_ends(jax.random.randint(keys[2], (LOANS,), 0, REG_BLOCK), jax.random.fold_in(keys[2], 1), 0, REG_BLOCK - 1).astype(jnp.int32),
        "block_pools": draw_block_pools(jax.random.fold_in(keys[11], 71), 0),
        "pool_slot": draw_pool_slot(jax.random.fold_in(keys[11], 71), 0),
        "init_state": set_ends(jax.random.randint(keys[5], (LOANS,), 0, LIVE), jax.random.fold_in(keys[5], 1), 0, LIVE - 1).astype(jnp.int32),
        "balance": jnp.clip(jnp.exp(math.log(2.0) - 1.3862944 * jax.random.uniform(keys[6], (LOANS,), jnp.float32) ** level_of(keys[6], (LOANS,), ((0, 8),), -0.2, 0.2)), 0.5, 2.0),
        "loan_to_value": jnp.clip(jnp.exp(math.log(1.3) - 0.9555114 * jax.random.uniform(keys[7], (LOANS,), jnp.float32) ** level_of(keys[7], (LOANS,), ((0, 8),), -0.2, 0.2)), 0.5, 1.3),
        "hazard_base": jnp.clip(jax.random.uniform(keys[8], (2, LIVE), jnp.float32, -4.0, -1.0), -4.0, -1.0),
        "hazard_slope": jnp.clip(jax.random.uniform(keys[9], (2, LIVE), jnp.float32, 1.0, 4.0), 1.0, 4.0),
        "attach_bps": draw_attach_bps(jax.random.fold_in(keys[11], 71), 0),
    }


stress_scale = 0.3


def roll_months(routed, path_place, path_count, log_value, initial, balance, hazard_base, hazard_slope):
    months = routed.shape[0]
    month_place = (jnp.arange(months, dtype=jnp.float32) + 1.0) / months
    stress_path = stress_scale * ((path_place + 0.5) / path_count)[None, :, None] * month_place[:, None, None]
    cumulated = jnp.cumsum(routed, axis=0) - stress_path
    level = log_value[None, None, :] - cumulated
    start_state = jnp.broadcast_to(initial[:, None, :], (initial.shape[0], routed.shape[1], routed.shape[2]))
    loss_start = jnp.zeros(routed.shape[1:], jnp.float32)

    def month_step(state_pair, ltv_now):
        state, loss_sum = state_pair
        roll_rate = jax.nn.sigmoid(hazard_base[0][:, None, None] + hazard_slope[0][:, None, None] * ltv_now[None])
        cure_rate = jax.nn.sigmoid(hazard_base[1][:, None, None] - hazard_slope[1][:, None, None] * ltv_now[None])
        stay_rate = (1.0 - roll_rate) * (1.0 - cure_rate)
        forward = state * roll_rate
        backward = state * (1.0 - roll_rate) * cure_rate
        first_state = state[0] * stay_rate[0] + jnp.sum(backward[1:], axis=0)
        rest_state = forward[:-1] + state[1:] * stay_rate[1:]
        updated = jnp.concatenate([first_state[None], rest_state], axis=0)
        severity = 0.1 + 0.5 * jax.nn.sigmoid(3.0 * ltv_now)
        loss_next = loss_sum + balance[None, :] * severity * forward[-1]
        return (updated, loss_next), loss_next

    state_pair, history = lax.scan(month_step, (start_state, loss_start), level)
    return history[3::4]


def tranche_shares(pool_loss, notional, attach_bps):
    pool_count = pool_loss.shape[0]
    attach = attach_bps.astype(jnp.float32) / 10000.0
    detach = jnp.concatenate([attach[:, 1:], jnp.ones((pool_count, 1), jnp.float32)], axis=1)
    ratio = pool_loss.reshape(pool_count, DATES, -1) / notional[:, None, None]
    lower = attach.T[:, :, None, None]
    height = (detach - attach).T[:, :, None, None]
    return jnp.clip((ratio[None] - lower) / height, 0.0, 1.0)


def reference(price_moves, block_regions, region_slot, block_pools, pool_slot, init_state, balance, loan_to_value, hazard_base, hazard_slope, attach_bps):
    block_index = (jnp.arange(LOANS, dtype=jnp.int32) // BLOCK).astype(jnp.int32)
    metro_id = block_regions[block_index, region_slot]
    pool_id = block_pools[block_index, pool_slot]
    log_value = jnp.log(loan_to_value)
    initial = (init_state[None, :] == jnp.arange(LIVE, dtype=jnp.int32)[:, None]).astype(jnp.float32)
    notional = jax.ops.segment_sum(balance, pool_id, POOLS)

    def one_block(block_number):
        first = (block_number * PATH_DEV).astype(jnp.int32)
        moves = lax.dynamic_slice_in_dim(price_moves, first, PATH_DEV, 2)
        routed = jnp.take(moves, metro_id, axis=1).astype(jnp.float32).transpose(0, 2, 1)
        path_place = (first + jnp.arange(PATH_DEV, dtype=jnp.int32)).astype(jnp.float32)
        losses = roll_months(routed, path_place, float(PATHS), log_value, initial, balance, hazard_base, hazard_slope)
        loss_rows = losses.reshape(DATES * PATH_DEV, LOANS).T
        pool_loss = jax.ops.segment_sum(loss_rows, pool_id, POOLS)
        shares = tranche_shares(pool_loss, notional, attach_bps)
        return jnp.sum(shares, axis=3).transpose(0, 2, 1), shares[:, :, -1, :]

    sums, lasts = lax.map(one_block, jnp.arange(N_PATH, dtype=jnp.int32))
    expected_loss = jnp.sum(sums, axis=0) / PATHS
    path_loss = lasts.transpose(1, 2, 0, 3).reshape(TRANCHES, POOLS, PATHS)
    return expected_loss, path_loss
```

```python
import functools

import jax
import jax.numpy as jnp
from jax import lax
from jax.experimental import pallas as pl
from jax.experimental.pallas import tpu as pltpu
from jax.sharding import PartitionSpec as P

BLOCK = 256
LANES = 128
STRESS = 0.3
F32 = jnp.float32
BF16 = jnp.bfloat16

VMEM = pl.BlockSpec(memory_space=pltpu.VMEM)
SMEM = pl.BlockSpec(memory_space=pltpu.SMEM)


def next_pow2(value):
    return 1 << (value - 1).bit_length()


class Sizes:
    def __init__(self, price_moves, block_regions, block_pools, attach_bps, hazard_base):
        self.devs = lax.axis_size("loan")
        self.path_devs = lax.axis_size("path")
        self.months, self.metros, self.paths = price_moves.shape
        self.blocks, self.regions = block_regions.shape
        self.slots = block_pools.shape[1]
        self.pools, self.tranches = attach_bps.shape
        self.live = hazard_base.shape[1]
        self.dates = self.months // 4
        self.width = self.paths // self.devs
        self.halves = 2
        self.half = self.width // self.halves
        self.pad = next_pow2(max(self.metros, 16))
        self.fold = LANES // self.pad
        self.groups = -(-self.months // self.fold)
        self.price_rows = self.groups * self.width
        self.loan_rows = self.blocks * BLOCK // LANES
        self.info_rows = -(-(10 * self.loan_rows + 2) // 16) * 16
        self.rows = self.price_rows + self.info_rows
        self.dev_slots = self.blocks * self.slots
        self.sources = LANES // self.dev_slots
        self.all_pools = self.pools * self.devs


def pieces(value, count):
    out = []
    for _ in range(count):
        piece = value.astype(BF16).astype(F32)
        out.append(piece)
        value = value - piece
    return out


def pack_kernel(z, moves, regions, pool_lists, region, pool, init, balance, ltv, out, info, table):
    me = lax.axis_index("loan")
    for g in range(z.groups):
        parts = []
        for h in range(z.fold):
            t = h * z.groups + g
            if t < z.months:
                block = moves[t].astype(F32)
            else:
                block = jnp.zeros((z.metros, z.paths), F32)
            parts.append(block)
            if z.pad > z.metros:
                parts.append(jnp.zeros((z.pad - z.metros, z.paths), F32))
        turned = jnp.concatenate(parts, axis=0).T
        step = z.paths // z.halves
        for k in range(z.devs):
            both = [turned[h * step + k * z.half : h * step + (k + 1) * z.half] for h in range(z.halves)]
            out[k, g * z.width : (g + 1) * z.width, :] = jnp.concatenate(both, axis=0).astype(BF16)
    info[...] = jnp.zeros_like(info)
    per = BLOCK // LANES
    for b in range(z.blocks):
        rows = slice(b * per, (b + 1) * per)
        slot = region[rows, :]
        metro = jnp.zeros(slot.shape, jnp.int32)
        for j in range(z.regions):
            metro = jnp.where(slot == j, regions[b, j], metro)
        owner = jnp.zeros(slot.shape, jnp.int32)
        for k in range(1, z.devs):
            owner = owner + jnp.where(metro >= k * z.metros, 1, 0)
        local = metro - owner * z.metros
        values = [owner.astype(F32), local.astype(F32), init[rows, :].astype(F32), pool[rows, :].astype(F32)]
        values += pieces(jnp.log(ltv[rows, :]), 3) + pieces(balance[rows, :], 3)
        for q, value in enumerate(values):
            info[q * z.loan_rows + b * per : q * z.loan_rows + (b + 1) * per, :] = value
    table[...] = jnp.zeros_like(table)
    table[0 : z.blocks, 0 : z.slots] = pool_lists[...].astype(F32)
    lists = table[...]
    row = lists[0:1, :]
    for b in range(1, z.blocks):
        row = row + pltpu.roll(lists, b * z.slots, 1)[b : b + 1, :]
    place = lax.broadcasted_iota(jnp.int32, (1, LANES), 1) // z.dev_slots
    wide = row
    for c in range(1, z.sources):
        wide = wide + pltpu.roll(jnp.broadcast_to(row, (8, LANES)), c * z.dev_slots, 1)[0:1, :]
    wide = jnp.where(place == lax.rem(me, z.sources), wide, 0.0)
    high = jnp.floor(wide * (1.0 / 64.0))
    info[10 * z.loan_rows : 10 * z.loan_rows + 1, :] = high
    info[10 * z.loan_rows + 1 : 10 * z.loan_rows + 2, :] = wide - 64.0 * high
    packed = info[...].astype(BF16)
    for k in range(z.devs):
        out[k, z.price_rows :, :] = packed


def rolled(value, shift):
    shift = shift % LANES
    return value if shift == 0 else pltpu.roll(value, shift, 1)


def months_kernel(z, got, base, slope, out, source_moves, moved, dated, sums, pool_rows, turned):
    lane = lax.broadcasted_iota(jnp.int32, (1, LANES), 1)
    for j in range(z.devs // z.fold):
        for h in range(z.fold):
            mixed = None
            count = min(z.groups, z.months - h * z.groups) * z.width
            if count <= 0:
                continue
            for i in range(z.fold):
                part = rolled(got[j * z.fold + i, 0 : z.price_rows, :].astype(F32), (i - h) * z.pad)
                mixed = part if mixed is None else jnp.where(lane // z.pad == i, part, mixed)
            source_moves[
                h * z.price_rows : h * z.price_rows + count, j * LANES : (j + 1) * LANES
            ] = mixed[0:count].astype(BF16)
    sums[...] = jnp.zeros_like(sums)
    pool_rows[...] = jnp.zeros_like(pool_rows)
    keys = z.devs * z.pad
    total_paths = z.paths * z.path_devs
    path = lax.broadcasted_iota(jnp.int32, (z.width, BLOCK), 0)
    here = (
        lax.axis_index("path") * z.paths
        + (path // z.half) * (z.paths // z.halves)
        + lax.axis_index("loan") * z.half
        + path % z.half
    )
    stress = STRESS * ((here.astype(F32) + 0.5) / float(total_paths)) / float(z.months)
    roll_base = [0.5 * base[0, s] for s in range(z.live)]
    roll_slope = [0.5 * slope[0, s] for s in range(z.live)]
    cure_base = [0.5 * base[1, s] for s in range(z.live)]
    cure_slope = [-0.5 * slope[1, s] for s in range(z.live)]
    per = BLOCK // LANES
    marks = z.dates * z.width

    def source_step(s, carry):
        info = got[s, z.price_rows :, :].astype(F32)
        group = s // z.sources
        pool_rows[group] = pool_rows[group] + info[10 * z.loan_rows : 10 * z.loan_rows + 2, :]

        for b in range(z.blocks):

            def row(q):
                first = q * z.loan_rows + b * per
                return jnp.concatenate([info[first + r : first + r + 1, :] for r in range(per)], axis=1)

            key = row(0) * float(z.pad) + row(1)
            iota = lax.broadcasted_iota(jnp.int32, (keys, BLOCK), 0).astype(F32)
            chooser = jnp.where(iota == key, 1.0, 0.0).astype(BF16)
            moved[...] = jnp.dot(source_moves[...], chooser, preferred_element_type=F32)
            start = row(2)
            balance_rows = [row(7), row(8), row(9)]
            balance = balance_rows[0] + balance_rows[1] + balance_rows[2]
            level = jnp.broadcast_to(row(4) + row(5) + row(6), (z.width, BLOCK))
            state = [
                jnp.broadcast_to(jnp.where(start == float(k), 1.0, 0.0), (z.width, BLOCK))
                for k in range(z.live)
            ]
            loss = jnp.zeros((z.width, BLOCK), F32)
            for t in range(z.months):
                level = level + (stress - moved[t * z.width : (t + 1) * z.width, :])
                ahead = []
                keep = []
                back = None
                for k in range(z.live):
                    roll = jnp.tanh(roll_base[k] + roll_slope[k] * level)
                    cure = jnp.tanh(cure_base[k] + cure_slope[k] * level)
                    part = state[k] * roll
                    ahead.append(state[k] + part)
                    rest = state[k] - part
                    cured = rest * cure
                    keep.append(rest - cured)
                    if k > 0:
                        gain = rest + cured
                        back = gain if back is None else back + gain
                scale = 0.5 * 0.25**t
                severity = 0.35 * scale + (0.25 * scale) * jnp.tanh(1.5 * level)
                loss = loss + severity * ahead[z.live - 1]
                state = [keep[0] + back] + [
                    2.0 * ahead[k - 1] + keep[k] for k in range(1, z.live)
                ]
                if t % 4 == 3:
                    d = t // 4
                    high, low = pieces(balance * loss, 2)
                    dated[d * z.width : (d + 1) * z.width, :] = high.astype(BF16)
                    dated[marks + d * z.width : marks + (d + 1) * z.width, :] = low.astype(BF16)
            money = jnp.concatenate(balance_rows + [jnp.zeros((13, BLOCK), F32)], axis=0)
            dated[2 * marks :, :] = money.astype(BF16)
            place = lax.rem(s, z.sources) * z.dev_slots + b * z.slots
            slot = row(3) + place.astype(F32)
            slot_iota = lax.broadcasted_iota(jnp.int32, (LANES, BLOCK), 0).astype(F32)
            members = jnp.where(slot_iota == slot, 1.0, 0.0).astype(BF16)
            sums[group] = sums[group] + lax.dot_general(
                dated[...], members, (((1,), (1,)), ((), ())), preferred_element_type=F32
            )
        return carry

    lax.fori_loop(0, z.devs, source_step, 0)

    for group in range(z.devs // z.sources):
        total = sums[group]
        money = total[2 * marks : 2 * marks + 1] + total[2 * marks + 1 : 2 * marks + 2]
        money = money + total[2 * marks + 2 : 2 * marks + 3]
        ratio = (total[0:marks] + total[marks : 2 * marks]) / money
        split = jnp.concatenate(pieces(ratio, 3), axis=0).astype(BF16)
        listed = pool_rows[group]
        pool_id = listed[0:1] * 64.0 + listed[1:2]
        pool_iota = lax.broadcasted_iota(jnp.int32, (z.all_pools, LANES), 0).astype(F32)
        order = jnp.where(pool_iota == pool_id, 1.0, 0.0).astype(BF16)
        part = lax.dot_general(
            split, order, (((1,), (1,)), ((), ())), preferred_element_type=F32
        )
        turned[...] = part if group == 0 else turned[...] + part
    ratio = turned[0:marks, :] + turned[marks : 2 * marks, :] + turned[2 * marks : 3 * marks, :]
    wide = LANES // z.pools
    for k in range(z.devs):
        both = ratio[:, (k // wide) * LANES : (k // wide + 1) * LANES]
        own = k % wide
        for d in range(z.dates):
            mixed = None
            for h in range(z.halves):
                first = d * z.width + h * z.half
                part = rolled(both[first : first + z.half], (h - own) * z.pools)
                mixed = part if mixed is None else jnp.where(lane // z.pools == h, part, mixed)
            out[k, d * z.half : (d + 1) * z.half, :] = mixed


def steps_of(z, bps):
    attach = bps.astype(F32) / 10000.0
    top = jnp.concatenate([attach[:, 1:], jnp.ones((z.pools, 1), F32)], axis=1)
    return attach, top - attach


def means_kernel(z, got, bps, out, scratch):
    attach, height = steps_of(z, bps[...])
    scratch[...] = jnp.zeros_like(scratch)
    scratch[0 : z.pools, 0 : z.tranches] = attach
    scratch[0 : z.pools, 8 : 8 + z.tranches] = height
    for h in range(1, z.halves):
        scratch[h * z.pools : (h + 1) * z.pools, 0:16] = scratch[0 : z.pools, 0:16]
    rows = scratch[...].T
    out[...] = jnp.zeros_like(out)
    for d in range(z.dates):
        ratio = jnp.concatenate(
            [got[k, d * z.half : (d + 1) * z.half, :] for k in range(z.devs)], axis=0
        )
        for j in range(z.tranches):
            share = jnp.clip((ratio - rows[j : j + 1]) / rows[8 + j : 9 + j], 0.0, 1.0)
            out[j * z.dates + d : j * z.dates + d + 1, :] = jnp.sum(share, axis=0, keepdims=True)


def paths_kernel(z, got, bps, out):
    attach, height = steps_of(z, bps[...])
    d = z.dates - 1
    ratio = jnp.concatenate(
        [got[k, d * z.half : (d + 1) * z.half, :] for k in range(z.devs)], axis=0
    )
    side = z.paths // z.halves
    turned = ratio.T
    ratio = jnp.concatenate(
        [turned[h * z.pools : (h + 1) * z.pools, 0:side] for h in range(z.halves)], axis=1
    )
    for j in range(z.tranches):
        share = (ratio - attach[:, j : j + 1]) / height[:, j : j + 1]
        out[j] = jnp.clip(share, 0.0, 1.0)


def shards(
    price_moves,
    block_regions,
    region_slot,
    block_pools,
    pool_slot,
    init_state,
    balance,
    loan_to_value,
    hazard_base,
    hazard_slope,
    attach_bps,
):
    z = Sizes(price_moves, block_regions, block_pools, attach_bps, hazard_base)

    def lanes(value):
        return value.reshape(z.loan_rows, LANES)

    sent = pl.pallas_call(
        functools.partial(pack_kernel, z),
        out_shape=jax.ShapeDtypeStruct((z.devs, z.rows, LANES), BF16),
        in_specs=[VMEM, SMEM] + [VMEM] * 6,
        out_specs=VMEM,
        scratch_shapes=[pltpu.VMEM((z.info_rows, LANES), F32), pltpu.VMEM((8, LANES), F32)],
        name="pack",
    )(
        price_moves,
        block_regions,
        block_pools,
        lanes(region_slot),
        lanes(pool_slot),
        lanes(init_state),
        lanes(balance),
        lanes(loan_to_value),
    )
    got = lax.all_to_all(sent, "loan", 0, 0, tiled=True)
    marks = z.dates * z.width
    slot_groups = z.devs // z.sources
    ratios = pl.pallas_call(
        functools.partial(months_kernel, z),
        out_shape=jax.ShapeDtypeStruct((z.devs, z.dates * z.half, LANES), F32),
        in_specs=[VMEM, SMEM, SMEM],
        out_specs=VMEM,
        scratch_shapes=[
            pltpu.VMEM((z.months * z.width, z.devs * z.pad), BF16),
            pltpu.VMEM((z.months * z.width, BLOCK), F32),
            pltpu.VMEM((2 * marks + 16, BLOCK), BF16),
            pltpu.VMEM((slot_groups, 2 * marks + 16, LANES), F32),
            pltpu.VMEM((slot_groups, 2, LANES), F32),
            pltpu.VMEM((3 * marks, z.all_pools), F32),
        ],
        name="months",
    )(got, hazard_base, hazard_slope)
    owned = lax.all_to_all(ratios, "loan", 0, 0, tiled=True)
    total_rows = -(-z.tranches * z.dates // 8) * 8
    sums = pl.pallas_call(
        functools.partial(means_kernel, z),
        out_shape=jax.ShapeDtypeStruct((total_rows, LANES), F32),
        in_specs=[VMEM, VMEM],
        out_specs=VMEM,
        scratch_shapes=[pltpu.VMEM((LANES, LANES), F32)],
        name="means",
    )(owned, attach_bps)
    terms = [sums] + [
        lax.ppermute(sums, "path", [(i, i ^ k) for i in range(z.path_devs)])
        for k in range(1, z.path_devs)
    ]
    path_loss = pl.pallas_call(
        functools.partial(paths_kernel, z),
        out_shape=jax.ShapeDtypeStruct((z.tranches, z.pools, z.paths), F32),
        in_specs=[VMEM, VMEM],
        out_specs=VMEM,
        name="paths",
    )(owned, attach_bps)
    while len(terms) > 1:
        terms = [terms[i] + terms[i + 1] for i in range(0, len(terms), 2)]
    total = terms[0][: z.tranches * z.dates]
    total = sum(total[:, h * z.pools : (h + 1) * z.pools] for h in range(z.halves))
    expected_loss = (total / (z.paths * z.path_devs)).reshape(z.tranches, z.dates, z.pools)
    return expected_loss, path_loss


def solution(mesh):
    in_specs = (
        P(None, "loan", "path"),
        P("loan", None),
        P("loan"),
        P("loan", None),
        P("loan"),
        P("loan"),
        P("loan"),
        P("loan"),
        P(),
        P(),
        P("loan", None),
    )
    out_specs = (P(None, None, "loan"), P(None, "loan", "path"))
    return jax.shard_map(shards, mesh=mesh, in_specs=in_specs, out_specs=out_specs, check_vma=False)
```

```python
import functools

import jax
import jax.numpy as jnp
from jax import lax
from jax.experimental import pallas as pl
from jax.experimental.pallas import tpu as pltpu
from jax.sharding import PartitionSpec as P

BLOCK = 256
LANES = 128
STRESS = 0.3
F32 = jnp.float32
BF16 = jnp.bfloat16

VMEM = pl.BlockSpec(memory_space=pltpu.VMEM)
SMEM = pl.BlockSpec(memory_space=pltpu.SMEM)


def next_pow2(value):
    return 1 << (value - 1).bit_length()


class Sizes:
    def __init__(self, price_moves, block_regions, block_pools, attach_bps, hazard_base):
        self.devs = lax.axis_size("loan")
        self.path_devs = lax.axis_size("path")
        self.chips = self.devs // 2
        self.months, self.metros, self.paths = price_moves.shape
        self.blocks, self.regions = block_regions.shape
        self.slots = block_pools.shape[1]
        self.pools, self.tranches = attach_bps.shape
        self.live = hazard_base.shape[1]
        self.dates = self.months // 4
        self.width = self.paths // self.devs
        self.halves = 2
        self.half = self.width // self.halves
        self.side = self.paths // self.halves
        self.pad = next_pow2(max(self.metros, 16))
        self.fold = LANES // self.pad
        self.groups = -(-self.months // self.fold)
        self.price_rows = self.groups * self.width
        self.per = BLOCK // LANES
        self.loan_rows = self.blocks * self.per
        self.list_row = 7 * self.loan_rows
        self.info_rows = -(-(self.list_row + 4) // 16) * 16
        self.rows = self.price_rows + self.info_rows
        self.dev_slots = self.blocks * self.slots
        self.sources = LANES // self.dev_slots
        self.all_pools = self.pools * self.devs
        self.slot_groups = self.devs // self.sources
        self.out_rows = self.dates * self.half
        self.steps = self.months * self.width

    def reach(self, state):
        return self.months - (self.live - 1 - state)


def pieces(value, count):
    out = []
    for _ in range(count):
        piece = value.astype(BF16).astype(F32)
        out.append(piece)
        value = value - piece
    return out


def rolled(value, shift):
    shift = shift % LANES
    return value if shift == 0 else pltpu.roll(value, shift, 1)


def pack_kernel(z, *refs):
    sources, (kept, passed), scratch = refs[:8], refs[8:10], refs[10:]
    moves, regions, pool_lists, region, pool, init, balance, ltv = scratch[:8]
    turned, info, table, arrived = scratch[8:]
    copies = [
        pltpu.make_async_copy(source, target, arrived.at[i])
        for i, (source, target) in enumerate(zip(sources, scratch[:8]))
    ]
    for copy in copies:
        copy.start()
    for copy in copies:
        copy.wait()
    me = lax.axis_index("loan")
    for g in range(z.groups):
        parts = []
        for h in range(z.fold):
            t = h * z.groups + g
            if t < z.months:
                parts.append(moves[t].astype(F32))
            else:
                parts.append(jnp.zeros((z.metros, z.paths), F32))
            if z.pad > z.metros:
                parts.append(jnp.zeros((z.pad - z.metros, z.paths), F32))
        turned[g] = jnp.concatenate(parts, axis=0).T
    for c in range(z.chips):
        for other, out in enumerate((kept, passed)):
            to = me ^ (2 * c + other)
            for g in range(z.groups):
                both = [
                    turned[g, pl.ds(h * z.side + to * z.half, z.half), :] for h in range(z.halves)
                ]
                first = c * z.rows + g * z.width
                out[first : first + z.width, :] = jnp.concatenate(both, axis=0).astype(BF16)
    info[...] = jnp.zeros_like(info)
    values = [region[...].astype(F32), init[...].astype(F32), pool[...].astype(F32)]
    values += pieces(jnp.log(ltv[...]), 2) + pieces(balance[...], 2)
    for q, value in enumerate(values):
        info[q * z.loan_rows : (q + 1) * z.loan_rows, :] = value
    lane = lax.broadcasted_iota(jnp.int32, (1, LANES), 1)
    mine = lane // z.dev_slots == lax.rem(me, z.sources)

    def spread(lists):
        table[...] = jnp.zeros_like(table)
        table[0 : z.blocks, 0 : z.slots] = lists.astype(F32)
        wide = table[...]
        row = wide[0:1, :]
        for b in range(1, z.blocks):
            row = row + pltpu.roll(wide, b * z.slots, 1)[b : b + 1, :]
        wide = row
        for c in range(1, z.sources):
            wide = wide + pltpu.roll(jnp.broadcast_to(row, (8, LANES)), c * z.dev_slots, 1)[0:1, :]
        return jnp.where(mine, wide, 0.0)

    listed = spread(pool_lists[...])
    high = jnp.floor(listed * (1.0 / 64.0))
    metro = spread(regions[...])
    owner = jnp.zeros_like(metro)
    for k in range(1, z.devs):
        owner = owner + jnp.where(metro >= float(k * z.metros), 1.0, 0.0)
    rows = [high, listed - 64.0 * high, owner, metro - owner * float(z.metros)]
    for i, row in enumerate(rows):
        info[z.list_row + i : z.list_row + i + 1, :] = row
    packed = info[...].astype(BF16)
    for c in range(z.chips):
        kept[c * z.rows + z.price_rows : (c + 1) * z.rows, :] = packed
        passed[c * z.rows + z.price_rows : (c + 1) * z.rows, :] = packed


def pair_kernel(z, rows, kept, passed, *outs):
    for c in range(1, z.chips):
        outs[c - 1][0:rows, :] = kept[c * rows : (c + 1) * rows, :]
        outs[c - 1][rows : 2 * rows, :] = passed[c * rows : (c + 1) * rows, :]


def part_of(z, own, others, j, rows):
    c, other = j // 2, j % 2
    if c == 0:
        return own[other], 0
    return others[c - 1], other * rows


def months_kernel(z, *refs):
    own, others = refs[:2], refs[2 : z.chips + 1]
    base, slope, kept, passed = refs[z.chips + 1 : z.chips + 5]
    (
        source_moves,
        info,
        both_pieces,
        moved_even,
        moved_odd,
        dated,
        sums,
        lists,
        ratios,
    ) = refs[z.chips + 5 :]
    me = lax.axis_index("loan")
    lane = lax.broadcasted_iota(jnp.int32, (1, LANES), 1)

    for j in range(z.devs // z.fold):
        parts = []
        for i in range(z.fold):
            ref, first = part_of(z, own, others, j * z.fold + i, z.rows)
            parts.append(ref[first : first + z.price_rows, :].astype(F32))
        for h in range(z.fold):
            mixed = None
            count = min(z.groups, z.months - h * z.groups) * z.width
            if count <= 0:
                continue
            for i in range(z.fold):
                part = rolled(parts[i], (i - h) * z.pad)
                mixed = part if mixed is None else jnp.where(lane // z.pad == i, part, mixed)
            first = h * z.price_rows
            source_moves[first : first + count, j * LANES : (j + 1) * LANES] = mixed[
                0:count
            ].astype(BF16)
    for j in range(z.devs):
        ref, first = part_of(z, own, others, j, z.rows)
        info[j] = ref[first + z.price_rows : first + z.rows, :].astype(F32)
    for group in range(z.slot_groups):
        total = info[group * z.sources, z.list_row : z.list_row + 4, :]
        for i in range(1, z.sources):
            total = total + info[group * z.sources + i, z.list_row : z.list_row + 4, :]
        lists[group] = total

    keys = z.devs * z.pad
    path = lax.broadcasted_iota(jnp.int32, (z.width, LANES), 0)
    here = (
        lax.axis_index("path") * z.paths
        + (path // z.half) * z.side
        + me * z.half
        + path % z.half
    )
    total_paths = float(z.paths * z.path_devs)
    stress = STRESS * ((here.astype(F32) + 0.5) / total_paths) / float(z.months)
    key_row = lax.broadcasted_iota(jnp.int32, (keys, LANES), 0).astype(F32)
    for group in range(z.slot_groups):
        listed = lists[group].astype(jnp.int32)
        key = ((listed[2:3] ^ me) * z.pad + listed[3:4]).astype(F32)
        chooser = jnp.where(key_row == key, 1.0, 0.0).astype(BF16)
        moved = jnp.dot(source_moves[...], chooser, preferred_element_type=F32)
        level = jnp.zeros((z.width, LANES), F32)
        highs, lows = [], []
        for t in range(z.months):
            level = level + (stress - moved[t * z.width : (t + 1) * z.width])
            high, low = pieces(level, 2)
            highs.append(high)
            lows.append(low)
        both_pieces[group, :, 0:LANES] = jnp.concatenate(highs, axis=0).astype(BF16)
        both_pieces[group, :, LANES:] = jnp.concatenate(lows, axis=0).astype(BF16)
    roll_base = [0.5 * base[0, k] for k in range(z.live)]
    roll_rate = [0.5 * slope[0, k] for k in range(z.live)]
    cure_base = [0.5 * base[1, k] for k in range(z.live)]
    cure_rate = [-0.5 * slope[1, k] for k in range(z.live)]
    sums[...] = jnp.zeros_like(sums)
    marks = z.dates * z.width
    slot_row = lax.broadcasted_iota(jnp.int32, (z.regions, BLOCK), 0).astype(F32)

    def row(j, b, q):
        first = q * z.loan_rows + b * z.per
        both = info[j, first : first + z.per, :]
        return jnp.concatenate([both[r : r + 1, :] for r in range(z.per)], axis=1)

    def one_hot(j, b, q):
        ours = jnp.where(slot_row == row(j, b, q), 1.0, 0.0)
        place = lax.rem(me ^ j, z.sources)
        parts = []
        for i in range(z.sources):
            here = jnp.where(place == i, ours, 0.0).astype(BF16)
            parts += [here if k == b else jnp.zeros_like(here) for k in range(z.blocks)]
        return jnp.concatenate(parts, axis=0)

    def fill(j, b, moved):
        chosen = one_hot(j, b, 0)
        chosen = jnp.concatenate([chosen, chosen], axis=0)
        moved[...] = jnp.dot(both_pieces[j // z.sources], chosen, preferred_element_type=F32)

    def run(j, b, moved):
        start = row(j, b, 1)
        begins = [start == float(k) for k in range(z.live)]
        ltv = row(j, b, 3) + row(j, b, 4)
        balance_rows = [row(j, b, q) for q in (5, 6)]
        balance = balance_rows[0] + balance_rows[1]

        def of_start(values):
            chosen = jnp.full((1, BLOCK), values[0], F32)
            for k in range(1, z.live):
                chosen = jnp.where(begins[k], values[k], chosen)
            return chosen

        state = None
        loss = jnp.zeros((z.width, BLOCK), F32)
        for t in range(z.months):
            level = moved[t * z.width : (t + 1) * z.width, :] + ltv
            ahead, keep, gain = [None] * z.live, [None] * z.live, [None] * z.live
            following = [None] * z.live
            if t == 0:
                size = of_start([0.5**k for k in range(z.live)])
                roll = size * jnp.tanh(of_start(roll_base) + of_start(roll_rate) * level)
                cure = jnp.tanh(of_start(cure_base) + of_start(cure_rate) * level)
                on = size + roll
                rest = size - roll
                cured = rest * cure
                stays = rest - cured
                back = of_start([1.0] + [2.0**k for k in range(1, z.live)]) * (rest + cured)
                ahead[z.live - 1] = jnp.where(begins[z.live - 1], on, 0.0)
                for k in range(1, z.live):
                    moves = jnp.where(begins[k - 1], on, 0.0)
                    following[k] = jnp.where(begins[k], stays, moves)
                following[0] = jnp.where(begins[0], stays, back)
            else:
                for k in range(z.live):
                    if t >= z.reach(k):
                        continue
                    part = state[k] * jnp.tanh(roll_base[k] + roll_rate[k] * level)
                    ahead[k] = state[k] + part
                    if t + 1 < z.reach(k):
                        rest = state[k] - part
                        cured = rest * jnp.tanh(cure_base[k] + cure_rate[k] * level)
                        keep[k] = rest - cured
                        gain[k] = rest + cured
                for k in range(1, z.live):
                    if t + 1 < z.reach(k):
                        following[k] = ahead[k - 1] + keep[k]
                if t + 1 < z.reach(0):
                    back = gain[z.live - 1]
                    for k in range(z.live - 2, 0, -1):
                        back = 2.0 * back + gain[k]
                    following[0] = keep[0] + 2.0 * back
            severity = jnp.tanh(1.5 * level)
            scale = 0.5 * 2.0 ** (z.live - 1) * 0.25**t
            loss = loss + (0.35 * scale + (0.25 * scale) * severity) * ahead[z.live - 1]
            state = following
            if t % 4 == 3:
                d = t // 4
                high, low = pieces(balance * loss, 2)
                dated[d * z.width : (d + 1) * z.width, :] = high.astype(BF16)
                dated[marks + d * z.width : marks + (d + 1) * z.width, :] = low.astype(BF16)
        money = jnp.concatenate(balance_rows + [jnp.zeros((14, BLOCK), F32)], axis=0)
        dated[2 * marks :, :] = money.astype(BF16)
        group = j // z.sources
        sums[group] = sums[group] + lax.dot_general(
            dated[...], one_hot(j, b, 2), (((1,), (1,)), ((), ())), preferred_element_type=F32
        )

    moved = (moved_even, moved_odd)

    def source_step(j, carry):
        for b in range(z.blocks):
            fill(j, b, moved[b % 2])
        for b in range(z.blocks):
            run(j, b, moved[b % 2])
        return carry

    lax.fori_loop(0, z.devs, source_step, 0)

    for group in range(z.slot_groups):
        total = sums[group]
        money = total[2 * marks : 2 * marks + 1] + total[2 * marks + 1 : 2 * marks + 2]
        ratio = (total[0:marks] + total[marks : 2 * marks]) / money
        split = jnp.concatenate(pieces(ratio, 3), axis=0).astype(BF16)
        listed = lists[group]
        pool_id = listed[0:1] * 64.0 + listed[1:2]
        pool_iota = lax.broadcasted_iota(jnp.int32, (z.all_pools, LANES), 0).astype(F32)
        order = jnp.where(pool_iota == pool_id, 1.0, 0.0).astype(BF16)
        part = lax.dot_general(
            split, order, (((1,), (1,)), ((), ())), preferred_element_type=F32
        )
        part = part[0:marks] + part[marks : 2 * marks] + part[2 * marks :]
        ratios[...] = part if group == 0 else ratios[...] + part
    for c in range(z.chips):
        to = me ^ (2 * c)
        both = ratios[:, pl.ds(pl.multiple_of((to * z.pools // LANES) * LANES, LANES), LANES)]
        for d in range(z.dates):
            made = []
            for own in range(LANES // z.pools):
                mixed = None
                for h in range(z.halves):
                    first = d * z.width + h * z.half
                    part = rolled(both[first : first + z.half], (h - own) * z.pools)
                    mixed = part if mixed is None else jnp.where(lane // z.pools == h, part, mixed)
                made.append(mixed)
            odd = lax.rem(me, 2) == 1
            rows = slice(c * z.out_rows + d * z.half, c * z.out_rows + (d + 1) * z.half)
            kept[rows, :] = jnp.where(odd, made[1], made[0])
            passed[rows, :] = jnp.where(odd, made[0], made[1])


def owned_ratio(z, own, others, j, d):
    ref, first = part_of(z, own, others, j, z.out_rows)
    return ref[first + d * z.half : first + (d + 1) * z.half, :]


def means_kernel(z, *refs):
    own, others, (bps, out, scratch) = refs[:2], refs[2 : z.chips + 1], refs[z.chips + 1 :]
    scratch[...] = jnp.zeros_like(scratch)
    scratch[0 : z.tranches, 0 : z.pools] = bps[...].astype(F32) / 10000.0
    rows = scratch[...]
    for h in range(1, z.halves):
        rows = rows + pltpu.roll(scratch[...], h * z.pools, 1)
    out[...] = jnp.zeros_like(out)
    for d in range(z.dates):
        ratio = jnp.concatenate(
            [owned_ratio(z, own, others, j, d) for j in range(z.devs)], axis=0
        )
        for j in range(z.tranches):
            low = rows[j : j + 1]
            height = (rows[j + 1 : j + 2] if j + 1 < z.tranches else 1.0) - low
            share = jnp.clip((ratio - low) / height, 0.0, 1.0)
            out[j * z.dates + d : j * z.dates + d + 1, :] = jnp.sum(share, axis=0, keepdims=True)


def paths_kernel(z, *refs):
    own, others = refs[:2], refs[2 : z.chips + 1]
    bps, out, scratch, columns = refs[z.chips + 1 :]
    me = lax.axis_index("loan")
    columns[...] = jnp.zeros_like(columns)
    columns[0 : z.tranches, 0 : z.pools] = bps[...].astype(F32) / 10000.0
    attach = columns[...].T
    for j in range(z.devs):
        first = (me ^ j) * z.half
        scratch[pl.ds(first, z.half), :] = owned_ratio(z, own, others, j, z.dates - 1)
    turned = scratch[...].T
    ratio = jnp.concatenate(
        [turned[h * z.pools : (h + 1) * z.pools, 0 : z.side] for h in range(z.halves)], axis=1
    )
    for j in range(z.tranches):
        low = attach[0 : z.pools, j : j + 1]
        high = attach[0 : z.pools, j + 1 : j + 2] if j + 1 < z.tranches else 1.0
        out[j] = jnp.clip((ratio - low) / (high - low), 0.0, 1.0)


def total_kernel(z, left, right, out):
    total = left[...] + right[...]
    wide = total
    for h in range(1, z.halves):
        wide = wide + pltpu.roll(total, LANES - h * z.pools, 1)
    wide = wide[:, 0 : z.pools] / float(z.paths * z.path_devs)
    for j in range(z.tranches):
        out[j] = wide[j * z.dates : (j + 1) * z.dates]


def grant(mib):
    return pltpu.CompilerParams(vmem_limit_bytes=mib << 20)


def exchange(z, kept, passed, rows):
    got = lax.ppermute(passed, "loan", [(i, i ^ 1) for i in range(z.devs)])
    pairs = pl.pallas_call(
        functools.partial(pair_kernel, z, rows),
        out_shape=[jax.ShapeDtypeStruct((2 * rows, LANES), kept.dtype)] * (z.chips - 1),
        in_specs=[VMEM] * 2,
        out_specs=[VMEM] * (z.chips - 1),
        compiler_params=grant(4),
        name="pair",
    )(kept, got)
    others = [
        lax.ppermute(pairs[c - 1], "loan", [(i, i ^ (2 * c)) for i in range(z.devs)])
        for c in range(1, z.chips)
    ]
    return [kept, got] + others


def shards(
    price_moves,
    block_regions,
    region_slot,
    block_pools,
    pool_slot,
    init_state,
    balance,
    loan_to_value,
    hazard_base,
    hazard_slope,
    attach_bps,
):
    z = Sizes(price_moves, block_regions, block_pools, attach_bps, hazard_base)

    def lanes(value):
        return value.reshape(z.loan_rows, LANES)

    inputs = [
        price_moves,
        block_regions,
        block_pools,
        lanes(region_slot),
        lanes(pool_slot),
        lanes(init_state),
        lanes(balance),
        lanes(loan_to_value),
    ]
    kept, passed = pl.pallas_call(
        functools.partial(pack_kernel, z),
        out_shape=[jax.ShapeDtypeStruct((z.chips * z.rows, LANES), BF16)] * 2,
        in_specs=[pl.BlockSpec(memory_space=pltpu.HBM)] * 8,
        out_specs=[VMEM] * 2,
        scratch_shapes=[pltpu.VMEM(value.shape, value.dtype) for value in inputs]
        + [
            pltpu.VMEM((z.groups, LANES, LANES), F32),
            pltpu.VMEM((z.info_rows, LANES), F32),
            pltpu.VMEM((8, LANES), F32),
            pltpu.SemaphoreType.DMA((8,)),
        ],
        compiler_params=grant(8),
        name="pack",
    )(*[pltpu.with_memory_space_constraint(value, pltpu.HBM) for value in inputs])
    parts = exchange(z, kept, passed, z.rows)
    marks = z.dates * z.width
    moved = pltpu.VMEM((z.steps, BLOCK), F32)
    kept, passed = pl.pallas_call(
        functools.partial(months_kernel, z),
        out_shape=[jax.ShapeDtypeStruct((z.chips * z.out_rows, LANES), F32)] * 2,
        in_specs=[VMEM] * (z.chips + 1) + [SMEM] * 2,
        out_specs=[VMEM] * 2,
        scratch_shapes=[
            pltpu.VMEM((z.steps, z.devs * z.pad), BF16),
            pltpu.VMEM((z.devs, z.info_rows, LANES), F32),
            pltpu.VMEM((z.slot_groups, z.steps, 2 * LANES), BF16),
            moved,
            moved,
            pltpu.VMEM((2 * marks + 16, BLOCK), BF16),
            pltpu.VMEM((z.slot_groups, 2 * marks + 16, LANES), F32),
            pltpu.VMEM((z.slot_groups, 4, LANES), F32),
            pltpu.VMEM((marks, z.all_pools), F32),
        ],
        compiler_params=grant(16),
        name="months",
    )(*parts, hazard_base, hazard_slope)
    parts = exchange(z, kept, passed, z.out_rows)
    attach = attach_bps.T
    total_rows = -(-z.tranches * z.dates // 8) * 8
    sums = pl.pallas_call(
        functools.partial(means_kernel, z),
        out_shape=jax.ShapeDtypeStruct((total_rows, LANES), F32),
        in_specs=[VMEM] * (z.chips + 2),
        out_specs=VMEM,
        scratch_shapes=[pltpu.VMEM((8, LANES), F32)],
        compiler_params=grant(4),
        name="means",
    )(*parts, attach)
    distance = 1
    while 2 * distance < z.path_devs:
        sums = sums + lax.ppermute(sums, "path", [(i, i ^ distance) for i in range(z.path_devs)])
        distance *= 2
    other = lax.ppermute(sums, "path", [(i, i ^ distance) for i in range(z.path_devs)])
    path_loss = pl.pallas_call(
        functools.partial(paths_kernel, z),
        out_shape=jax.ShapeDtypeStruct((z.tranches, z.pools, z.paths), F32),
        in_specs=[VMEM] * (z.chips + 2),
        out_specs=VMEM,
        scratch_shapes=[pltpu.VMEM((z.side, LANES), F32), pltpu.VMEM((8, LANES), F32)],
        compiler_params=grant(4),
        name="paths",
    )(*parts, attach)
    expected_loss = pl.pallas_call(
        functools.partial(total_kernel, z),
        out_shape=jax.ShapeDtypeStruct((z.tranches, z.dates, z.pools), F32),
        in_specs=[VMEM] * 2,
        out_specs=VMEM,
        compiler_params=grant(4),
        name="total",
    )(sums, other)
    return expected_loss, path_loss


def solution(mesh):
    in_specs = (
        P(None, "loan", "path"),
        P("loan", None),
        P("loan"),
        P("loan", None),
        P("loan"),
        P("loan"),
        P("loan"),
        P("loan"),
        P(),
        P(),
        P("loan", None),
    )
    out_specs = (P(None, None, "loan"), P(None, "loan", "path"))
    return jax.shard_map(shards, mesh=mesh, in_specs=in_specs, out_specs=out_specs, check_vma=False)
```

```python
import functools

import jax
import jax.numpy as jnp
from jax import lax
from jax.experimental import pallas as pl
from jax.experimental.pallas import tpu as pltpu
from jax.sharding import PartitionSpec as P

BLOCK = 256
LANES = 128
STRESS = 0.3
F32 = jnp.float32
BF16 = jnp.bfloat16

VMEM = pl.BlockSpec(memory_space=pltpu.VMEM)
SMEM = pl.BlockSpec(memory_space=pltpu.SMEM)


def next_pow2(value):
    return 1 << (value - 1).bit_length()


class Sizes:
    def __init__(self, price_moves, block_regions, block_pools, attach_bps, hazard_base):
        self.devs = lax.axis_size("loan")
        self.path_devs = lax.axis_size("path")
        self.chips = self.devs // 2
        self.months, self.metros, self.paths = price_moves.shape
        self.blocks, self.regions = block_regions.shape
        self.slots = block_pools.shape[1]
        self.pools, self.tranches = attach_bps.shape
        self.live = hazard_base.shape[1]
        self.dates = self.months // 4
        self.width = self.paths // self.devs
        self.halves = 2
        self.half = self.width // self.halves
        self.side = self.paths // self.halves
        self.pad = next_pow2(max(self.metros, 16))
        self.fold = LANES // self.pad
        self.groups = -(-self.months // self.fold)
        self.price_rows = self.groups * self.width
        self.per = BLOCK // LANES
        self.loan_rows = self.blocks * self.per
        self.list_row = 7 * self.loan_rows
        self.info_rows = -(-(self.list_row + 4) // 16) * 16
        self.rows = self.price_rows + self.info_rows
        self.sent_rows = self.price_rows + self.rows
        self.dev_slots = self.blocks * self.slots
        self.sources = LANES // self.dev_slots
        self.all_pools = self.pools * self.devs
        self.slot_groups = self.devs // self.sources
        self.out_rows = self.dates * self.half
        self.steps = self.months * self.width

    def reach(self, state):
        return self.months - (self.live - 1 - state)


def pieces(value, count):
    out = []
    for _ in range(count):
        piece = value.astype(BF16).astype(F32)
        out.append(piece)
        value = value - piece
    return out


def rolled(value, shift):
    shift = shift % LANES
    return value if shift == 0 else pltpu.roll(value, shift, 1)


def pack_kernel(z, *refs):
    sources, outs, scratch = refs[:8], refs[8 : 8 + z.chips], refs[8 + z.chips :]
    moves, regions, pool_lists, region, pool, init, balance, ltv = scratch[:8]
    turned, info, table, arrived = scratch[8:]
    copies = [
        pltpu.make_async_copy(source, target, arrived.at[i])
        for i, (source, target) in enumerate(zip(sources, scratch[:8]))
    ]
    for copy in copies:
        copy.start()
    for copy in copies:
        copy.wait()
    me = lax.axis_index("loan")
    for g in range(z.groups):
        parts = []
        for h in range(z.fold):
            t = h * z.groups + g
            if t < z.months:
                parts.append(moves[t].astype(F32))
            else:
                parts.append(jnp.zeros((z.metros, z.paths), F32))
            if z.pad > z.metros:
                parts.append(jnp.zeros((z.pad - z.metros, z.paths), F32))
        turned[g] = jnp.concatenate(parts, axis=0).T
    for c in range(z.chips):
        for other in range(2):
            to = me ^ (2 * c + other)
            for g in range(z.groups):
                both = [
                    turned[g, pl.ds(h * z.side + to * z.half, z.half), :] for h in range(z.halves)
                ]
                first = other * z.price_rows + g * z.width
                outs[c][first : first + z.width, :] = jnp.concatenate(both, axis=0).astype(BF16)
    info[...] = jnp.zeros_like(info)
    values = [region[...].astype(F32), init[...].astype(F32), pool[...].astype(F32)]
    values += pieces(jnp.log(ltv[...]), 2) + pieces(balance[...], 2)
    for q, value in enumerate(values):
        info[q * z.loan_rows : (q + 1) * z.loan_rows, :] = value
    lane = lax.broadcasted_iota(jnp.int32, (1, LANES), 1)
    mine = lane // z.dev_slots == lax.rem(me, z.sources)

    def spread(lists):
        table[...] = jnp.zeros_like(table)
        table[0 : z.blocks, 0 : z.slots] = lists.astype(F32)
        wide = table[...]
        row = wide[0:1, :]
        for b in range(1, z.blocks):
            row = row + pltpu.roll(wide, b * z.slots, 1)[b : b + 1, :]
        wide = row
        for c in range(1, z.sources):
            wide = wide + pltpu.roll(jnp.broadcast_to(row, (8, LANES)), c * z.dev_slots, 1)[0:1, :]
        return jnp.where(mine, wide, 0.0)

    listed = spread(pool_lists[...])
    high = jnp.floor(listed * (1.0 / 64.0))
    metro = spread(regions[...])
    owner = jnp.zeros_like(metro)
    for k in range(1, z.devs):
        owner = owner + jnp.where(metro >= float(k * z.metros), 1.0, 0.0)
    rows = [high, listed - 64.0 * high, owner, metro - owner * float(z.metros)]
    for i, row in enumerate(rows):
        info[z.list_row + i : z.list_row + i + 1, :] = row
    packed = info[...].astype(BF16)
    for c in range(z.chips):
        outs[c][2 * z.price_rows :, :] = packed


def pass_kernel(z, rows, *refs):
    parts, out = refs[:-1], refs[-1]
    for c, part in enumerate(parts):
        out[c * rows : (c + 1) * rows, :] = part[part.shape[0] - rows :, :]


def months_kernel(z, *refs):
    near, (far, base, slope), outs = (
        refs[: z.chips],
        refs[z.chips : z.chips + 3],
        refs[z.chips + 3 : 2 * z.chips + 3],
    )
    (
        source_moves,
        info,
        both_pieces,
        moved_even,
        moved_odd,
        dated,
        sums,
        lists,
        ratios,
    ) = refs[2 * z.chips + 3 :]
    me = lax.axis_index("loan")
    lane = lax.broadcasted_iota(jnp.int32, (1, LANES), 1)

    def prices_of(j):
        c = j // 2
        if j % 2 == 0:
            return near[c][0 : z.price_rows, :]
        return far[c * z.rows : c * z.rows + z.price_rows, :]

    for j in range(z.devs // z.fold):
        parts = []
        for i in range(z.fold):
            parts.append(prices_of(j * z.fold + i).astype(F32))
        for h in range(z.fold):
            mixed = None
            count = min(z.groups, z.months - h * z.groups) * z.width
            if count <= 0:
                continue
            for i in range(z.fold):
                part = rolled(parts[i], (i - h) * z.pad)
                mixed = part if mixed is None else jnp.where(lane // z.pad == i, part, mixed)
            first = h * z.price_rows
            source_moves[first : first + count, j * LANES : (j + 1) * LANES] = mixed[
                0:count
            ].astype(BF16)
    for j in range(z.devs):
        c = j // 2
        if j % 2 == 0:
            part = near[c][2 * z.price_rows :, :]
        else:
            part = far[c * z.rows + z.price_rows : (c + 1) * z.rows, :]
        info[j] = part.astype(F32)
    for group in range(z.slot_groups):
        total = info[group * z.sources, z.list_row : z.list_row + 4, :]
        for i in range(1, z.sources):
            total = total + info[group * z.sources + i, z.list_row : z.list_row + 4, :]
        lists[group] = total

    keys = z.devs * z.pad
    path = lax.broadcasted_iota(jnp.int32, (z.width, LANES), 0)
    here = (
        lax.axis_index("path") * z.paths
        + (path // z.half) * z.side
        + me * z.half
        + path % z.half
    )
    total_paths = float(z.paths * z.path_devs)
    stress = STRESS * ((here.astype(F32) + 0.5) / total_paths) / float(z.months)
    key_row = lax.broadcasted_iota(jnp.int32, (keys, LANES), 0).astype(F32)
    for group in range(z.slot_groups):
        listed = lists[group].astype(jnp.int32)
        key = ((listed[2:3] ^ me) * z.pad + listed[3:4]).astype(F32)
        chooser = jnp.where(key_row == key, 1.0, 0.0).astype(BF16)
        moved = jnp.dot(source_moves[...], chooser, preferred_element_type=F32)
        level = jnp.zeros((z.width, LANES), F32)
        highs, lows = [], []
        for t in range(z.months):
            level = level + (stress - moved[t * z.width : (t + 1) * z.width])
            high, low = pieces(level, 2)
            highs.append(high)
            lows.append(low)
        both_pieces[group, :, 0:LANES] = jnp.concatenate(highs, axis=0).astype(BF16)
        both_pieces[group, :, LANES:] = jnp.concatenate(lows, axis=0).astype(BF16)
    roll_base = [0.5 * base[0, k] for k in range(z.live)]
    roll_rate = [0.5 * slope[0, k] for k in range(z.live)]
    cure_base = [0.5 * base[1, k] for k in range(z.live)]
    cure_rate = [-0.5 * slope[1, k] for k in range(z.live)]
    sums[...] = jnp.zeros_like(sums)
    marks = z.dates * z.width
    slot_row = lax.broadcasted_iota(jnp.int32, (z.regions, BLOCK), 0).astype(F32)

    def row(j, b, q):
        first = q * z.loan_rows + b * z.per
        both = info[j, first : first + z.per, :]
        return jnp.concatenate([both[r : r + 1, :] for r in range(z.per)], axis=1)

    def one_hot(j, b, q):
        ours = jnp.where(slot_row == row(j, b, q), 1.0, 0.0)
        place = lax.rem(me ^ j, z.sources)
        parts = []
        for i in range(z.sources):
            here = jnp.where(place == i, ours, 0.0).astype(BF16)
            parts += [here if k == b else jnp.zeros_like(here) for k in range(z.blocks)]
        return jnp.concatenate(parts, axis=0)

    def fill(j, b, moved):
        chosen = one_hot(j, b, 0)
        chosen = jnp.concatenate([chosen, chosen], axis=0)
        moved[...] = jnp.dot(both_pieces[j // z.sources], chosen, preferred_element_type=F32)

    def run(j, b, moved):
        start = row(j, b, 1)
        begins = [start == float(k) for k in range(z.live)]
        ltv = row(j, b, 3) + row(j, b, 4)
        balance_rows = [row(j, b, q) for q in (5, 6)]
        balance = balance_rows[0] + balance_rows[1]

        def of_start(values):
            chosen = jnp.full((1, BLOCK), values[0], F32)
            for k in range(1, z.live):
                chosen = jnp.where(begins[k], values[k], chosen)
            return chosen

        state = None
        loss = jnp.zeros((z.width, BLOCK), F32)
        for t in range(z.months):
            level = moved[t * z.width : (t + 1) * z.width, :] + ltv
            ahead, keep, gain = [None] * z.live, [None] * z.live, [None] * z.live
            following = [None] * z.live
            if t == 0:
                size = of_start([0.5**k for k in range(z.live)])
                roll = size * jnp.tanh(of_start(roll_base) + of_start(roll_rate) * level)
                cure = jnp.tanh(of_start(cure_base) + of_start(cure_rate) * level)
                on = size + roll
                rest = size - roll
                cured = rest * cure
                stays = rest - cured
                back = of_start([1.0] + [2.0**k for k in range(1, z.live)]) * (rest + cured)
                ahead[z.live - 1] = jnp.where(begins[z.live - 1], on, 0.0)
                for k in range(1, z.live):
                    moves = jnp.where(begins[k - 1], on, 0.0)
                    following[k] = jnp.where(begins[k], stays, moves)
                following[0] = jnp.where(begins[0], stays, back)
            else:
                for k in range(z.live):
                    if t >= z.reach(k):
                        continue
                    part = state[k] * jnp.tanh(roll_base[k] + roll_rate[k] * level)
                    ahead[k] = state[k] + part
                    if t + 1 < z.reach(k):
                        rest = state[k] - part
                        cured = rest * jnp.tanh(cure_base[k] + cure_rate[k] * level)
                        keep[k] = rest - cured
                        gain[k] = rest + cured
                for k in range(1, z.live):
                    if t + 1 < z.reach(k):
                        following[k] = ahead[k - 1] + keep[k]
                if t + 1 < z.reach(0):
                    back = gain[z.live - 1]
                    for k in range(z.live - 2, 0, -1):
                        back = 2.0 * back + gain[k]
                    following[0] = keep[0] + 2.0 * back
            severity = jnp.tanh(1.5 * level)
            scale = 0.5 * 2.0 ** (z.live - 1) * 0.25**t
            loss = loss + (0.35 * scale + (0.25 * scale) * severity) * ahead[z.live - 1]
            state = following
            if t % 4 == 3:
                d = t // 4
                high, low = pieces(balance * loss, 2)
                dated[d * z.width : (d + 1) * z.width, :] = high.astype(BF16)
                dated[marks + d * z.width : marks + (d + 1) * z.width, :] = low.astype(BF16)
        money = jnp.concatenate(balance_rows + [jnp.zeros((14, BLOCK), F32)], axis=0)
        dated[2 * marks :, :] = money.astype(BF16)
        group = j // z.sources
        sums[group] = sums[group] + lax.dot_general(
            dated[...], one_hot(j, b, 2), (((1,), (1,)), ((), ())), preferred_element_type=F32
        )

    moved = (moved_even, moved_odd)

    def source_step(j, carry):
        for b in range(z.blocks):
            fill(j, b, moved[b % 2])
        for b in range(z.blocks):
            run(j, b, moved[b % 2])
        return carry

    lax.fori_loop(0, z.devs, source_step, 0)

    for group in range(z.slot_groups):
        total = sums[group]
        money = total[2 * marks : 2 * marks + 1] + total[2 * marks + 1 : 2 * marks + 2]
        ratio = (total[0:marks] + total[marks : 2 * marks]) / money
        split = jnp.concatenate(pieces(ratio, 3), axis=0).astype(BF16)
        listed = lists[group]
        pool_id = listed[0:1] * 64.0 + listed[1:2]
        pool_iota = lax.broadcasted_iota(jnp.int32, (z.all_pools, LANES), 0).astype(F32)
        order = jnp.where(pool_iota == pool_id, 1.0, 0.0).astype(BF16)
        part = lax.dot_general(
            split, order, (((1,), (1,)), ((), ())), preferred_element_type=F32
        )
        part = part[0:marks] + part[marks : 2 * marks] + part[2 * marks :]
        ratios[...] = part if group == 0 else ratios[...] + part
    for c in range(z.chips):
        to = me ^ (2 * c)
        both = ratios[:, pl.ds(pl.multiple_of((to * z.pools // LANES) * LANES, LANES), LANES)]
        for d in range(z.dates):
            made = []
            for own in range(LANES // z.pools):
                mixed = None
                for h in range(z.halves):
                    first = d * z.width + h * z.half
                    part = rolled(both[first : first + z.half], (h - own) * z.pools)
                    mixed = part if mixed is None else jnp.where(lane // z.pools == h, part, mixed)
                made.append(mixed)
            odd = lax.rem(me, 2) == 1
            rows = slice(d * z.half, (d + 1) * z.half)
            outs[c][rows, :] = jnp.where(odd, made[1], made[0])
            rows = slice(z.out_rows + d * z.half, z.out_rows + (d + 1) * z.half)
            outs[c][rows, :] = jnp.where(odd, made[0], made[1])


def owned_ratio(z, near, far, j, d):
    c = j // 2
    if j % 2 == 0:
        return near[c][d * z.half : (d + 1) * z.half, :]
    return far[c * z.out_rows + d * z.half : c * z.out_rows + (d + 1) * z.half, :]


def means_kernel(z, *refs):
    near, (far, bps, out, scratch) = refs[: z.chips], refs[z.chips :]
    scratch[...] = jnp.zeros_like(scratch)
    scratch[0 : z.tranches, 0 : z.pools] = bps[...].astype(F32) / 10000.0
    rows = scratch[...]
    for h in range(1, z.halves):
        rows = rows + pltpu.roll(scratch[...], h * z.pools, 1)
    out[...] = jnp.zeros_like(out)
    for d in range(z.dates):
        ratio = jnp.concatenate(
            [owned_ratio(z, near, far, j, d) for j in range(z.devs)], axis=0
        )
        for j in range(z.tranches):
            low = rows[j : j + 1]
            height = (rows[j + 1 : j + 2] if j + 1 < z.tranches else 1.0) - low
            share = jnp.clip((ratio - low) / height, 0.0, 1.0)
            out[j * z.dates + d : j * z.dates + d + 1, :] = jnp.sum(share, axis=0, keepdims=True)


def paths_kernel(z, *refs):
    near, (far, bps, out, scratch, columns) = refs[: z.chips], refs[z.chips :]
    me = lax.axis_index("loan")
    columns[...] = jnp.zeros_like(columns)
    columns[0 : z.tranches, 0 : z.pools] = bps[...].astype(F32) / 10000.0
    attach = columns[...].T
    for j in range(z.devs):
        first = (me ^ j) * z.half
        scratch[pl.ds(first, z.half), :] = owned_ratio(z, near, far, j, z.dates - 1)
    turned = scratch[...].T
    ratio = jnp.concatenate(
        [turned[h * z.pools : (h + 1) * z.pools, 0 : z.side] for h in range(z.halves)], axis=1
    )
    for j in range(z.tranches):
        low = attach[0 : z.pools, j : j + 1]
        high = attach[0 : z.pools, j + 1 : j + 2] if j + 1 < z.tranches else 1.0
        out[j] = jnp.clip((ratio - low) / (high - low), 0.0, 1.0)


def total_kernel(z, *refs):
    terms, out = [ref[...] for ref in refs[:-1]], refs[-1]
    while len(terms) > 1:
        terms = [terms[i] + terms[i + 1] for i in range(0, len(terms), 2)]
    total = terms[0]
    wide = total
    for h in range(1, z.halves):
        wide = wide + pltpu.roll(total, LANES - h * z.pools, 1)
    wide = wide[:, 0 : z.pools] / float(z.paths * z.path_devs)
    for j in range(z.tranches):
        out[j] = wide[j * z.dates : (j + 1) * z.dates]


def grant(mib):
    return pltpu.CompilerParams(vmem_limit_bytes=mib << 20)


def exchange(z, parts, rows):
    near = [parts[0]] + [None] * (z.chips - 1)
    for c in range(z.chips - 1, 0, -1):
        near[c] = lax.ppermute(parts[c], "loan", [(i, i ^ (2 * c)) for i in range(z.devs)])
    passed = pl.pallas_call(
        functools.partial(pass_kernel, z, rows),
        out_shape=jax.ShapeDtypeStruct((z.chips * rows, LANES), parts[0].dtype),
        in_specs=[VMEM] * z.chips,
        out_specs=VMEM,
        compiler_params=grant(4),
        name="pass",
    )(*near)
    return near + [lax.ppermute(passed, "loan", [(i, i ^ 1) for i in range(z.devs)])]


def shards(
    price_moves,
    block_regions,
    region_slot,
    block_pools,
    pool_slot,
    init_state,
    balance,
    loan_to_value,
    hazard_base,
    hazard_slope,
    attach_bps,
):
    z = Sizes(price_moves, block_regions, block_pools, attach_bps, hazard_base)

    def lanes(value):
        return value.reshape(z.loan_rows, LANES)

    inputs = [
        price_moves,
        block_regions,
        block_pools,
        lanes(region_slot),
        lanes(pool_slot),
        lanes(init_state),
        lanes(balance),
        lanes(loan_to_value),
    ]
    sent = pl.pallas_call(
        functools.partial(pack_kernel, z),
        out_shape=[jax.ShapeDtypeStruct((z.sent_rows, LANES), BF16)] * z.chips,
        in_specs=[pl.BlockSpec(memory_space=pltpu.HBM)] * 8,
        out_specs=[VMEM] * z.chips,
        scratch_shapes=[pltpu.VMEM(value.shape, value.dtype) for value in inputs]
        + [
            pltpu.VMEM((z.groups, LANES, LANES), F32),
            pltpu.VMEM((z.info_rows, LANES), F32),
            pltpu.VMEM((8, LANES), F32),
            pltpu.SemaphoreType.DMA((8,)),
        ],
        compiler_params=grant(8),
        name="pack",
    )(*[pltpu.with_memory_space_constraint(value, pltpu.HBM) for value in inputs])
    parts = exchange(z, sent, z.rows)
    marks = z.dates * z.width
    moved = pltpu.VMEM((z.steps, BLOCK), F32)
    sent = pl.pallas_call(
        functools.partial(months_kernel, z),
        out_shape=[jax.ShapeDtypeStruct((2 * z.out_rows, LANES), F32)] * z.chips,
        in_specs=[VMEM] * (z.chips + 1) + [SMEM] * 2,
        out_specs=[VMEM] * z.chips,
        scratch_shapes=[
            pltpu.VMEM((z.steps, z.devs * z.pad), BF16),
            pltpu.VMEM((z.devs, z.info_rows, LANES), F32),
            pltpu.VMEM((z.slot_groups, z.steps, 2 * LANES), BF16),
            moved,
            moved,
            pltpu.VMEM((2 * marks + 16, BLOCK), BF16),
            pltpu.VMEM((z.slot_groups, 2 * marks + 16, LANES), F32),
            pltpu.VMEM((z.slot_groups, 4, LANES), F32),
            pltpu.VMEM((marks, z.all_pools), F32),
        ],
        compiler_params=grant(16),
        name="months",
    )(*parts, hazard_base, hazard_slope)
    parts = exchange(z, sent, z.out_rows)
    attach = attach_bps.T
    total_rows = -(-z.tranches * z.dates // 8) * 8
    sums = pl.pallas_call(
        functools.partial(means_kernel, z),
        out_shape=jax.ShapeDtypeStruct((total_rows, LANES), F32),
        in_specs=[VMEM] * (z.chips + 2),
        out_specs=VMEM,
        scratch_shapes=[pltpu.VMEM((8, LANES), F32)],
        compiler_params=grant(4),
        name="means",
    )(*parts, attach)
    terms = [sums] + [
        lax.ppermute(sums, "path", [(i, i ^ k) for i in range(z.path_devs)])
        for k in range(1, z.path_devs)
    ]
    path_loss = pl.pallas_call(
        functools.partial(paths_kernel, z),
        out_shape=jax.ShapeDtypeStruct((z.tranches, z.pools, z.paths), F32),
        in_specs=[VMEM] * (z.chips + 2),
        out_specs=VMEM,
        scratch_shapes=[pltpu.VMEM((z.side, LANES), F32), pltpu.VMEM((8, LANES), F32)],
        compiler_params=grant(4),
        name="paths",
    )(*parts, attach)
    expected_loss = pl.pallas_call(
        functools.partial(total_kernel, z),
        out_shape=jax.ShapeDtypeStruct((z.tranches, z.dates, z.pools), F32),
        in_specs=[VMEM] * z.path_devs,
        out_specs=VMEM,
        compiler_params=grant(4),
        name="total",
    )(*terms)
    return expected_loss, path_loss


def solution(mesh):
    in_specs = (
        P(None, "loan", "path"),
        P("loan", None),
        P("loan"),
        P("loan", None),
        P("loan"),
        P("loan"),
        P("loan"),
        P("loan"),
        P(),
        P(),
        P("loan", None),
    )
    out_specs = (P(None, None, "loan"), P(None, "loan", "path"))
    return jax.shard_map(shards, mesh=mesh, in_specs=in_specs, out_specs=out_specs, check_vma=False)
```

```python
import functools

import jax
import jax.numpy as jnp
from jax import lax
from jax.experimental import pallas as pl
from jax.experimental.pallas import tpu as pltpu
from jax.sharding import PartitionSpec as P

BLOCK = 256
LANES = 128
STRESS = 0.3
F32 = jnp.float32
BF16 = jnp.bfloat16

VMEM = pl.BlockSpec(memory_space=pltpu.VMEM)
SMEM = pl.BlockSpec(memory_space=pltpu.SMEM)


def next_pow2(value):
    return 1 << (value - 1).bit_length()


class Sizes:
    def __init__(self, price_moves, block_regions, block_pools, attach_bps, hazard_base):
        self.devs = lax.axis_size("loan")
        self.path_devs = lax.axis_size("path")
        self.chips = self.devs // 2
        self.months, self.metros, self.paths = price_moves.shape
        self.blocks, self.regions = block_regions.shape
        self.slots = block_pools.shape[1]
        self.pools, self.tranches = attach_bps.shape
        self.live = hazard_base.shape[1]
        self.dates = self.months // 4
        self.width = self.paths // self.devs
        self.halves = 2
        self.half = self.width // self.halves
        self.side = self.paths // self.halves
        self.pad = next_pow2(max(self.metros, 16))
        self.fold = LANES // self.pad
        self.groups = -(-self.months // self.fold)
        self.price_rows = self.groups * self.width
        self.per = BLOCK // LANES
        self.loan_rows = self.blocks * self.per
        self.list_row = 7 * self.loan_rows
        self.info_rows = -(-(self.list_row + 4) // 16) * 16
        self.rows = self.price_rows + self.info_rows
        self.sent_rows = self.price_rows + self.rows
        self.dev_slots = self.blocks * self.slots
        self.sources = LANES // self.dev_slots
        self.all_pools = self.pools * self.devs
        self.slot_groups = self.devs // self.sources
        self.out_rows = self.dates * self.half
        self.steps = self.months * self.width

    def reach(self, state):
        return self.months - (self.live - 1 - state)


def pieces(value, count):
    out = []
    for _ in range(count):
        piece = value.astype(BF16).astype(F32)
        out.append(piece)
        value = value - piece
    return out


def rolled(value, shift):
    shift = shift % LANES
    return value if shift == 0 else pltpu.roll(value, shift, 1)


def pack_kernel(z, *refs):
    sources, outs, scratch = refs[:8], refs[8 : 8 + z.chips], refs[8 + z.chips :]
    moves, regions, pool_lists, region, pool, init, balance, ltv = scratch[:8]
    turned, info, table, arrived = scratch[8:]
    copies = [
        pltpu.make_async_copy(source, target, arrived.at[i])
        for i, (source, target) in enumerate(zip(sources, scratch[:8]))
    ]
    for copy in copies:
        copy.start()
    for copy in copies:
        copy.wait()
    me = lax.axis_index("loan")
    for g in range(z.groups):
        parts = []
        for h in range(z.fold):
            t = h * z.groups + g
            if t < z.months:
                parts.append(moves[t].astype(F32))
            else:
                parts.append(jnp.zeros((z.metros, z.paths), F32))
            if z.pad > z.metros:
                parts.append(jnp.zeros((z.pad - z.metros, z.paths), F32))
        turned[g] = jnp.concatenate(parts, axis=0).T
    for c in range(z.chips):
        for other in range(2):
            to = me ^ (2 * c + other)
            for g in range(z.groups):
                both = [
                    turned[g, pl.ds(h * z.side + to * z.half, z.half), :] for h in range(z.halves)
                ]
                first = other * z.price_rows + g * z.width
                outs[c][first : first + z.width, :] = jnp.concatenate(both, axis=0).astype(BF16)
    info[...] = jnp.zeros_like(info)
    values = [region[...].astype(F32), init[...].astype(F32), pool[...].astype(F32)]
    values += pieces(jnp.log(ltv[...]), 2) + pieces(balance[...], 2)
    for q, value in enumerate(values):
        info[q * z.loan_rows : (q + 1) * z.loan_rows, :] = value
    lane = lax.broadcasted_iota(jnp.int32, (1, LANES), 1)
    mine = lane // z.dev_slots == lax.rem(me, z.sources)

    def spread(lists):
        table[...] = jnp.zeros_like(table)
        table[0 : z.blocks, 0 : z.slots] = lists.astype(F32)
        wide = table[...]
        row = wide[0:1, :]
        for b in range(1, z.blocks):
            row = row + pltpu.roll(wide, b * z.slots, 1)[b : b + 1, :]
        wide = row
        for c in range(1, z.sources):
            wide = wide + pltpu.roll(jnp.broadcast_to(row, (8, LANES)), c * z.dev_slots, 1)[0:1, :]
        return jnp.where(mine, wide, 0.0)

    listed = spread(pool_lists[...])
    high = jnp.floor(listed * (1.0 / 64.0))
    metro = spread(regions[...])
    owner = jnp.zeros_like(metro)
    for k in range(1, z.devs):
        owner = owner + jnp.where(metro >= float(k * z.metros), 1.0, 0.0)
    rows = [high, listed - 64.0 * high, owner, metro - owner * float(z.metros)]
    for i, row in enumerate(rows):
        info[z.list_row + i : z.list_row + i + 1, :] = row
    packed = info[...].astype(BF16)
    for c in range(z.chips):
        outs[c][2 * z.price_rows :, :] = packed


def pass_kernel(z, rows, *refs):
    parts, out = refs[:-1], refs[-1]
    for c, part in enumerate(parts):
        out[c * rows : (c + 1) * rows, :] = part[part.shape[0] - rows :, :]


def months_kernel(z, *refs):
    near, (far, base, slope), outs = (
        refs[: z.chips],
        refs[z.chips : z.chips + 3],
        refs[z.chips + 3 : 2 * z.chips + 3],
    )
    (
        source_moves,
        info,
        loans,
        both_pieces,
        moved_even,
        moved_odd,
        dated,
        sums,
        lists,
        ratios,
    ) = refs[2 * z.chips + 3 :]
    me = lax.axis_index("loan")
    lane = lax.broadcasted_iota(jnp.int32, (1, LANES), 1)

    def prices_of(j):
        c = j // 2
        if j % 2 == 0:
            return near[c][0 : z.price_rows, :]
        return far[c * z.rows : c * z.rows + z.price_rows, :]

    for j in range(z.devs // z.fold):
        parts = []
        for i in range(z.fold):
            parts.append(prices_of(j * z.fold + i).astype(F32))
        for h in range(z.fold):
            mixed = None
            count = min(z.groups, z.months - h * z.groups) * z.width
            if count <= 0:
                continue
            for i in range(z.fold):
                part = rolled(parts[i], (i - h) * z.pad)
                mixed = part if mixed is None else jnp.where(lane // z.pad == i, part, mixed)
            first = h * z.price_rows
            source_moves[first : first + count, j * LANES : (j + 1) * LANES] = mixed[
                0:count
            ].astype(BF16)
    for j in range(z.devs):
        c = j // 2
        if j % 2 == 0:
            part = near[c][2 * z.price_rows :, :]
        else:
            part = far[c * z.rows + z.price_rows : (c + 1) * z.rows, :]
        info[j] = part.astype(F32)
    for group in range(z.slot_groups):
        total = info[group * z.sources, z.list_row : z.list_row + 4, :]
        for i in range(1, z.sources):
            total = total + info[group * z.sources + i, z.list_row : z.list_row + 4, :]
        lists[group] = total

    keys = z.devs * z.pad
    path = lax.broadcasted_iota(jnp.int32, (z.width, LANES), 0)
    here = (
        lax.axis_index("path") * z.paths
        + (path // z.half) * z.side
        + me * z.half
        + path % z.half
    )
    total_paths = float(z.paths * z.path_devs)
    stress = STRESS * ((here.astype(F32) + 0.5) / total_paths) / float(z.months)
    key_row = lax.broadcasted_iota(jnp.int32, (keys, LANES), 0).astype(F32)
    for group in range(z.slot_groups):
        listed = lists[group].astype(jnp.int32)
        key = ((listed[2:3] ^ me) * z.pad + listed[3:4]).astype(F32)
        chooser = jnp.where(key_row == key, 1.0, 0.0).astype(BF16)
        moved = jnp.dot(source_moves[...], chooser, preferred_element_type=F32)
        level = jnp.zeros((z.width, LANES), F32)
        levels = []
        for t in range(z.months):
            level = level + (stress - moved[t * z.width : (t + 1) * z.width])
            levels.append(level)
        level = jnp.concatenate(levels, axis=0)
        high, low = pieces((0.5 * slope[0, z.live - 1]) * level, 2)
        both_pieces[group, :, 0:LANES] = high.astype(BF16)
        both_pieces[group, :, LANES:] = low.astype(BF16)
    last_base, last_rate = 0.5 * base[0, z.live - 1], 0.5 * slope[0, z.live - 1]
    roll_rate = [slope[0, k] / slope[0, z.live - 1] for k in range(z.live)]
    cure_rate = [-(slope[1, k] / slope[0, z.live - 1]) for k in range(z.live)]
    roll_base = [0.5 * base[0, k] - roll_rate[k] * last_base for k in range(z.live)]
    cure_base = [0.5 * base[1, k] - cure_rate[k] * last_base for k in range(z.live)]
    severity_rate = 3.0 / slope[0, z.live - 1]
    severity_base = -(severity_rate * last_base)
    for j in range(z.devs):
        rows = [info[j, q * z.loan_rows : (q + 1) * z.loan_rows, :] for q in range(7)]
        ltv = rows[3] + rows[4]

        def of_start(values):
            chosen = jnp.full(rows[1].shape, values[0], F32)
            for k in range(1, z.live):
                chosen = jnp.where(rows[1] == float(k), values[k], chosen)
            return chosen

        per_loan = [
            last_base + last_rate * ltv,
            rows[5] + rows[6],
            of_start([0.5**k for k in range(z.live)]),
            of_start([2.0**k for k in range(z.live)]),
        ]
        for rates in (roll_base, roll_rate, cure_base, cure_rate):
            per_loan.append(of_start(rates))
        for rates in (roll_base, roll_rate, cure_base, cure_rate):
            per_loan.append(of_start(rates[1:] + [0.0]))
        for q, value in enumerate(per_loan):
            loans[j, q * z.loan_rows : (q + 1) * z.loan_rows, :] = value
    sums[...] = jnp.zeros_like(sums)
    marks = z.dates * z.width
    slot_row = lax.broadcasted_iota(jnp.int32, (z.regions, BLOCK), 0).astype(F32)

    def row(j, b, q, values=info):
        first = q * z.loan_rows + b * z.per
        both = values[j, first : first + z.per, :]
        return jnp.concatenate([both[r : r + 1, :] for r in range(z.per)], axis=1)

    def one_hot(j, b, q):
        ours = jnp.where(slot_row == row(j, b, q), 1.0, 0.0)
        place = lax.rem(me ^ j, z.sources)
        parts = []
        for i in range(z.sources):
            here = jnp.where(place == i, ours, 0.0).astype(BF16)
            parts += [here if k == b else jnp.zeros_like(here) for k in range(z.blocks)]
        return jnp.concatenate(parts, axis=0)

    def fill(j, b, moved):
        chosen = one_hot(j, b, 0)
        chosen = jnp.concatenate([chosen, chosen], axis=0)
        moved[...] = jnp.dot(both_pieces[j // z.sources], chosen, preferred_element_type=F32)

    def run(j, b, moved):
        start = row(j, b, 1)
        begins = [start == float(k) for k in range(z.live)]
        balance_rows = [row(j, b, q) for q in (5, 6)]
        own_last, balance, size, power = [row(j, b, q, loans) for q in range(4)]
        rates = [row(j, b, q, loans) for q in range(4, 12)]
        top = z.live - 1

        def step(mass, roll_offset, roll_rate, cure_offset, cure_rate, x):
            part = mass * jnp.tanh(roll_offset + roll_rate * x)
            rest = mass - part
            cured = rest * jnp.tanh(cure_offset + cure_rate * x)
            return mass + part, rest - cured, rest + cured

        state = None
        loss = jnp.zeros((z.width, BLOCK), F32)
        for t in range(z.months):
            x = moved[t * z.width : (t + 1) * z.width, :] + own_last
            ahead, keep, gain = [None] * z.live, [None] * z.live, [None] * z.live
            following = [None] * z.live
            if t == 0:
                on, stays, back = step(size, *rates[:4], x)
                ahead[top] = jnp.where(begins[top], on, 0.0)
                following = [
                    stays,
                    jnp.where(begins[top], 0.0, on),
                    jnp.where(begins[0], 0.0, power * back),
                ]
            elif t == 1:
                on, stays, back = step(state[0], *rates[:4], x)
                next_on, next_stays, next_back = step(state[1], *rates[4:], x)
                first_on, first_stays, _ = step(
                    state[2], roll_base[0], roll_rate[0], cure_base[0], cure_rate[0], x
                )
                middle = on + next_stays
                ahead[top] = jnp.where(
                    begins[top], on, jnp.where(begins[top - 1], next_on, 0.0)
                )
                for k in range(1, z.live):
                    value = jnp.where(begins[k - 2], next_on, 0.0) if k > 1 else 0.0
                    value = jnp.where(begins[k - 1], middle, value)
                    following[k] = jnp.where(begins[k], stays, value)
                following[1] = following[1] + first_on
                own = jnp.where(begins[0], stays, power * back)
                following[0] = own + (2.0 * power) * next_back + first_stays
            else:
                for k in range(z.live):
                    if t >= z.reach(k):
                        continue
                    argument = x if k == top else roll_base[k] + roll_rate[k] * x
                    part = state[k] * jnp.tanh(argument)
                    ahead[k] = state[k] + part
                    if t + 1 < z.reach(k):
                        rest = state[k] - part
                        cured = rest * jnp.tanh(cure_base[k] + cure_rate[k] * x)
                        keep[k] = rest - cured
                        gain[k] = rest + cured
                for k in range(1, z.live):
                    if t + 1 < z.reach(k):
                        following[k] = ahead[k - 1] + keep[k]
                if t + 1 < z.reach(0):
                    back = gain[top]
                    for k in range(top - 1, 0, -1):
                        back = 2.0 * back + gain[k]
                    following[0] = keep[0] + 2.0 * back
            severity = jnp.tanh(severity_base + severity_rate * x)
            scale = 0.5 * 2.0 ** (z.live - 1) * 0.25**t
            loss = loss + (0.35 * scale + (0.25 * scale) * severity) * ahead[top]
            state = following
            if t % 4 == 3:
                d = t // 4
                high, low = pieces(balance * loss, 2)
                dated[d * z.width : (d + 1) * z.width, :] = high.astype(BF16)
                dated[marks + d * z.width : marks + (d + 1) * z.width, :] = low.astype(BF16)
        money = jnp.concatenate(balance_rows + [jnp.zeros((14, BLOCK), F32)], axis=0)
        dated[2 * marks :, :] = money.astype(BF16)
        group = j // z.sources
        sums[group] = sums[group] + lax.dot_general(
            dated[...], one_hot(j, b, 2), (((1,), (1,)), ((), ())), preferred_element_type=F32
        )

    moved = (moved_even, moved_odd)

    unroll = min(8, z.devs)

    def source_step(step, carry):
        order = [(step * unroll + i, b) for i in range(unroll) for b in range(z.blocks)]
        fill(*order[0], moved[0])
        for i, (j, b) in enumerate(order):
            if i + 1 < len(order):
                fill(*order[i + 1], moved[(i + 1) % 2])
            run(j, b, moved[i % 2])
        return carry

    lax.fori_loop(0, z.devs // unroll, source_step, 0)

    for group in range(z.slot_groups):
        total = sums[group]
        money = total[2 * marks : 2 * marks + 1] + total[2 * marks + 1 : 2 * marks + 2]
        ratio = (total[0:marks] + total[marks : 2 * marks]) / money
        split = jnp.concatenate(pieces(ratio, 3), axis=0).astype(BF16)
        listed = lists[group]
        pool_id = listed[0:1] * 64.0 + listed[1:2]
        pool_iota = lax.broadcasted_iota(jnp.int32, (z.all_pools, LANES), 0).astype(F32)
        order = jnp.where(pool_iota == pool_id, 1.0, 0.0).astype(BF16)
        part = lax.dot_general(
            split, order, (((1,), (1,)), ((), ())), preferred_element_type=F32
        )
        part = part[0:marks] + part[marks : 2 * marks] + part[2 * marks :]
        ratios[...] = part if group == 0 else ratios[...] + part
    for c in range(z.chips):
        to = me ^ (2 * c)
        both = ratios[:, pl.ds(pl.multiple_of((to * z.pools // LANES) * LANES, LANES), LANES)]
        for d in range(z.dates):
            made = []
            for own in range(LANES // z.pools):
                mixed = None
                for h in range(z.halves):
                    first = d * z.width + h * z.half
                    part = rolled(both[first : first + z.half], (h - own) * z.pools)
                    mixed = part if mixed is None else jnp.where(lane // z.pools == h, part, mixed)
                made.append(mixed)
            odd = lax.rem(me, 2) == 1
            rows = slice(d * z.half, (d + 1) * z.half)
            outs[c][rows, :] = jnp.where(odd, made[1], made[0])
            rows = slice(z.out_rows + d * z.half, z.out_rows + (d + 1) * z.half)
            outs[c][rows, :] = jnp.where(odd, made[0], made[1])


def owned_ratio(z, near, far, j, d):
    c = j // 2
    if j % 2 == 0:
        return near[c][d * z.half : (d + 1) * z.half, :]
    return far[c * z.out_rows + d * z.half : c * z.out_rows + (d + 1) * z.half, :]


def means_kernel(z, *refs):
    near, (far, bps, out, scratch) = refs[: z.chips], refs[z.chips :]
    scratch[...] = jnp.zeros_like(scratch)
    scratch[0 : z.tranches, 0 : z.pools] = bps[...].astype(F32) / 10000.0
    rows = scratch[...]
    for h in range(1, z.halves):
        rows = rows + pltpu.roll(scratch[...], h * z.pools, 1)
    out[...] = jnp.zeros_like(out)
    for d in range(z.dates):
        ratio = jnp.concatenate(
            [owned_ratio(z, near, far, j, d) for j in range(z.devs)], axis=0
        )
        for j in range(z.tranches):
            low = rows[j : j + 1]
            height = (rows[j + 1 : j + 2] if j + 1 < z.tranches else 1.0) - low
            share = jnp.clip((ratio - low) / height, 0.0, 1.0)
            out[j * z.dates + d : j * z.dates + d + 1, :] = jnp.sum(share, axis=0, keepdims=True)


def paths_kernel(z, *refs):
    near, (far, bps, out, scratch, columns) = refs[: z.chips], refs[z.chips :]
    me = lax.axis_index("loan")
    columns[...] = jnp.zeros_like(columns)
    columns[0 : z.tranches, 0 : z.pools] = bps[...].astype(F32) / 10000.0
    attach = columns[...].T
    for j in range(z.devs):
        first = (me ^ j) * z.half
        scratch[pl.ds(first, z.half), :] = owned_ratio(z, near, far, j, z.dates - 1)
    turned = scratch[...].T
    ratio = jnp.concatenate(
        [turned[h * z.pools : (h + 1) * z.pools, 0 : z.side] for h in range(z.halves)], axis=1
    )
    for j in range(z.tranches):
        low = attach[0 : z.pools, j : j + 1]
        high = attach[0 : z.pools, j + 1 : j + 2] if j + 1 < z.tranches else 1.0
        out[j] = jnp.clip((ratio - low) / (high - low), 0.0, 1.0)


def total_kernel(z, *refs):
    terms, out = [ref[...] for ref in refs[:-1]], refs[-1]
    while len(terms) > 1:
        terms = [terms[i] + terms[i + 1] for i in range(0, len(terms), 2)]
    total = terms[0]
    wide = total
    for h in range(1, z.halves):
        wide = wide + pltpu.roll(total, LANES - h * z.pools, 1)
    wide = wide[:, 0 : z.pools] / float(z.paths * z.path_devs)
    for j in range(z.tranches):
        out[j] = wide[j * z.dates : (j + 1) * z.dates]


def grant(mib):
    return pltpu.CompilerParams(vmem_limit_bytes=mib << 20)


def exchange(z, parts, rows):
    near = [parts[0]] + [None] * (z.chips - 1)
    for c in range(z.chips - 1, 0, -1):
        near[c] = lax.ppermute(parts[c], "loan", [(i, i ^ (2 * c)) for i in range(z.devs)])
    passed = pl.pallas_call(
        functools.partial(pass_kernel, z, rows),
        out_shape=jax.ShapeDtypeStruct((z.chips * rows, LANES), parts[0].dtype),
        in_specs=[VMEM] * z.chips,
        out_specs=VMEM,
        compiler_params=grant(4),
        name="pass",
    )(*near)
    return near + [lax.ppermute(passed, "loan", [(i, i ^ 1) for i in range(z.devs)])]


def shards(
    price_moves,
    block_regions,
    region_slot,
    block_pools,
    pool_slot,
    init_state,
    balance,
    loan_to_value,
    hazard_base,
    hazard_slope,
    attach_bps,
):
    z = Sizes(price_moves, block_regions, block_pools, attach_bps, hazard_base)

    def lanes(value):
        return value.reshape(z.loan_rows, LANES)

    inputs = [
        price_moves,
        block_regions,
        block_pools,
        lanes(region_slot),
        lanes(pool_slot),
        lanes(init_state),
        lanes(balance),
        lanes(loan_to_value),
    ]
    sent = pl.pallas_call(
        functools.partial(pack_kernel, z),
        out_shape=[jax.ShapeDtypeStruct((z.sent_rows, LANES), BF16)] * z.chips,
        in_specs=[pl.BlockSpec(memory_space=pltpu.HBM)] * 8,
        out_specs=[VMEM] * z.chips,
        scratch_shapes=[pltpu.VMEM(value.shape, value.dtype) for value in inputs]
        + [
            pltpu.VMEM((z.groups, LANES, LANES), F32),
            pltpu.VMEM((z.info_rows, LANES), F32),
            pltpu.VMEM((8, LANES), F32),
            pltpu.SemaphoreType.DMA((8,)),
        ],
        compiler_params=grant(8),
        name="pack",
    )(*[pltpu.with_memory_space_constraint(value, pltpu.HBM) for value in inputs])
    parts = exchange(z, sent, z.rows)
    marks = z.dates * z.width
    moved = pltpu.VMEM((z.steps, BLOCK), F32)
    sent = pl.pallas_call(
        functools.partial(months_kernel, z),
        out_shape=[jax.ShapeDtypeStruct((2 * z.out_rows, LANES), F32)] * z.chips,
        in_specs=[VMEM] * (z.chips + 1) + [SMEM] * 2,
        out_specs=[VMEM] * z.chips,
        scratch_shapes=[
            pltpu.VMEM((z.steps, z.devs * z.pad), BF16),
            pltpu.VMEM((z.devs, z.info_rows, LANES), F32),
            pltpu.VMEM((z.devs, 12 * z.loan_rows, LANES), F32),
            pltpu.VMEM((z.slot_groups, z.steps, 2 * LANES), BF16),
            moved,
            moved,
            pltpu.VMEM((2 * marks + 16, BLOCK), BF16),
            pltpu.VMEM((z.slot_groups, 2 * marks + 16, LANES), F32),
            pltpu.VMEM((z.slot_groups, 4, LANES), F32),
            pltpu.VMEM((marks, z.all_pools), F32),
        ],
        compiler_params=grant(16),
        name="months",
    )(*parts, hazard_base, hazard_slope)
    parts = exchange(z, sent, z.out_rows)
    attach = attach_bps.T
    total_rows = -(-z.tranches * z.dates // 8) * 8
    sums = pl.pallas_call(
        functools.partial(means_kernel, z),
        out_shape=jax.ShapeDtypeStruct((total_rows, LANES), F32),
        in_specs=[VMEM] * (z.chips + 2),
        out_specs=VMEM,
        scratch_shapes=[pltpu.VMEM((8, LANES), F32)],
        compiler_params=grant(4),
        name="means",
    )(*parts, attach)
    terms = [sums] + [
        lax.ppermute(sums, "path", [(i, i ^ k) for i in range(z.path_devs)])
        for k in range(1, z.path_devs)
    ]
    path_loss = pl.pallas_call(
        functools.partial(paths_kernel, z),
        out_shape=jax.ShapeDtypeStruct((z.tranches, z.pools, z.paths), F32),
        in_specs=[VMEM] * (z.chips + 2),
        out_specs=VMEM,
        scratch_shapes=[pltpu.VMEM((z.side, LANES), F32), pltpu.VMEM((8, LANES), F32)],
        compiler_params=grant(4),
        name="paths",
    )(*parts, attach)
    expected_loss = pl.pallas_call(
        functools.partial(total_kernel, z),
        out_shape=jax.ShapeDtypeStruct((z.tranches, z.dates, z.pools), F32),
        in_specs=[VMEM] * z.path_devs,
        out_specs=VMEM,
        compiler_params=grant(4),
        name="total",
    )(*terms)
    return expected_loss, path_loss


def solution(mesh):
    in_specs = (
        P(None, "loan", "path"),
        P("loan", None),
        P("loan"),
        P("loan", None),
        P("loan"),
        P("loan"),
        P("loan"),
        P("loan"),
        P(),
        P(),
        P("loan", None),
    )
    out_specs = (P(None, None, "loan"), P(None, "loan", "path"))
    return jax.shard_map(shards, mesh=mesh, in_specs=in_specs, out_specs=out_specs, check_vma=False)
```

```python
import functools

import jax
import jax.numpy as jnp
from jax import lax
from jax.experimental import pallas as pl
from jax.experimental.pallas import tpu as pltpu
from jax.sharding import PartitionSpec as P

BLOCK = 256
LANES = 128
STRESS = 0.3
F32 = jnp.float32
BF16 = jnp.bfloat16

VMEM = pl.BlockSpec(memory_space=pltpu.VMEM)
SMEM = pl.BlockSpec(memory_space=pltpu.SMEM)


def next_pow2(value):
    return 1 << (value - 1).bit_length()


class Sizes:
    def __init__(self, price_moves, block_regions, block_pools, attach_bps, hazard_base):
        self.devs = lax.axis_size("loan")
        self.path_devs = lax.axis_size("path")
        self.chips = self.devs // 2
        self.months, self.metros, self.paths = price_moves.shape
        self.blocks, self.regions = block_regions.shape
        self.slots = block_pools.shape[1]
        self.pools, self.tranches = attach_bps.shape
        self.live = hazard_base.shape[1]
        self.dates = self.months // 4
        self.width = self.paths // self.devs
        self.halves = 2
        self.half = self.width // self.halves
        self.side = self.paths // self.halves
        self.pad = next_pow2(max(self.metros, 16))
        self.fold = LANES // self.pad
        self.groups = -(-self.months // self.fold)
        self.price_rows = self.groups * self.width
        self.per = BLOCK // LANES
        self.loan_rows = self.blocks * self.per
        self.list_row = 7 * self.loan_rows
        self.info_rows = -(-(self.list_row + 4) // 16) * 16
        self.rows = self.price_rows + self.info_rows
        self.sent_rows = self.price_rows + self.rows
        self.dev_slots = self.blocks * self.slots
        self.sources = LANES // self.dev_slots
        self.all_pools = self.pools * self.devs
        self.slot_groups = self.devs // self.sources
        self.out_rows = self.dates * self.half
        self.steps = self.months * self.width

    def reach(self, state):
        return self.months - (self.live - 1 - state)


def pieces(value, count):
    out = []
    for _ in range(count):
        piece = value.astype(BF16).astype(F32)
        out.append(piece)
        value = value - piece
    return out


def rolled(value, shift):
    shift = shift % LANES
    return value if shift == 0 else pltpu.roll(value, shift, 1)


def pack_kernel(z, *refs):
    sources, outs, scratch = refs[:8], refs[8 : 8 + z.chips], refs[8 + z.chips :]
    moves, regions, pool_lists, region, pool, init, balance, ltv = scratch[:8]
    turned, info, table, arrived = scratch[8:]
    copies = [
        pltpu.make_async_copy(source, target, arrived.at[i])
        for i, (source, target) in enumerate(zip(sources, scratch[:8]))
    ]
    for copy in copies:
        copy.start()
    for copy in copies[1:]:
        copy.wait()
    me = lax.axis_index("loan")
    info[...] = jnp.zeros_like(info)
    values = [region[...].astype(F32), init[...].astype(F32), pool[...].astype(F32)]
    values += pieces(jnp.log(ltv[...]), 2) + pieces(balance[...], 2)
    for q, value in enumerate(values):
        info[q * z.loan_rows : (q + 1) * z.loan_rows, :] = value
    lane = lax.broadcasted_iota(jnp.int32, (1, LANES), 1)
    mine = lane // z.dev_slots == lax.rem(me, z.sources)

    def spread(lists):
        table[...] = jnp.zeros_like(table)
        table[0 : z.blocks, 0 : z.slots] = lists.astype(F32)
        wide = table[...]
        row = wide[0:1, :]
        for b in range(1, z.blocks):
            row = row + pltpu.roll(wide, b * z.slots, 1)[b : b + 1, :]
        wide = row
        for c in range(1, z.sources):
            wide = wide + pltpu.roll(jnp.broadcast_to(row, (8, LANES)), c * z.dev_slots, 1)[0:1, :]
        return jnp.where(mine, wide, 0.0)

    listed = spread(pool_lists[...])
    high = jnp.floor(listed * (1.0 / 64.0))
    metro = spread(regions[...])
    owner = jnp.zeros_like(metro)
    for k in range(1, z.devs):
        owner = owner + jnp.where(metro >= float(k * z.metros), 1.0, 0.0)
    rows = [high, listed - 64.0 * high, owner, metro - owner * float(z.metros)]
    for i, row in enumerate(rows):
        info[z.list_row + i : z.list_row + i + 1, :] = row
    packed = info[...].astype(BF16)
    for c in range(z.chips):
        outs[c][2 * z.price_rows :, :] = packed
    copies[0].wait()
    for g in range(z.groups):
        parts = []
        for h in range(z.fold):
            t = h * z.groups + g
            if t < z.months:
                parts.append(moves[t].astype(F32))
            else:
                parts.append(jnp.zeros((z.metros, z.paths), F32))
            if z.pad > z.metros:
                parts.append(jnp.zeros((z.pad - z.metros, z.paths), F32))
        turned[g] = jnp.concatenate(parts, axis=0).T
    for c in range(z.chips):
        for other in range(2):
            to = me ^ (2 * c + other)
            for g in range(z.groups):
                both = [
                    turned[g, pl.ds(h * z.side + to * z.half, z.half), :] for h in range(z.halves)
                ]
                first = other * z.price_rows + g * z.width
                outs[c][first : first + z.width, :] = jnp.concatenate(both, axis=0).astype(BF16)


def pass_kernel(z, rows, *refs):
    parts, out = refs[:-1], refs[-1]
    for c, part in enumerate(parts):
        out[c * rows : (c + 1) * rows, :] = part[part.shape[0] - rows :, :]


def months_kernel(z, *refs):
    near, (far, base, slope), outs = (
        refs[: z.chips],
        refs[z.chips : z.chips + 3],
        refs[z.chips + 3 : 2 * z.chips + 3],
    )
    (
        source_moves,
        info,
        loans,
        both_pieces,
        moved_even,
        moved_odd,
        dated,
        sums,
        lists,
        ratios,
    ) = refs[2 * z.chips + 3 :]
    me = lax.axis_index("loan")
    lane = lax.broadcasted_iota(jnp.int32, (1, LANES), 1)

    def prices_of(j):
        c = j // 2
        if j % 2 == 0:
            return near[c][0 : z.price_rows, :]
        return far[c * z.rows : c * z.rows + z.price_rows, :]

    for j in range(z.devs // z.fold):
        parts = []
        for i in range(z.fold):
            parts.append(prices_of(j * z.fold + i).astype(F32))
        for h in range(z.fold):
            mixed = None
            count = min(z.groups, z.months - h * z.groups) * z.width
            if count <= 0:
                continue
            for i in range(z.fold):
                part = rolled(parts[i], (i - h) * z.pad)
                mixed = part if mixed is None else jnp.where(lane // z.pad == i, part, mixed)
            first = h * z.price_rows
            source_moves[first : first + count, j * LANES : (j + 1) * LANES] = mixed[
                0:count
            ].astype(BF16)
    for j in range(z.devs):
        c = j // 2
        if j % 2 == 0:
            part = near[c][2 * z.price_rows :, :]
        else:
            part = far[c * z.rows + z.price_rows : (c + 1) * z.rows, :]
        info[j] = part.astype(F32)
    for group in range(z.slot_groups):
        total = info[group * z.sources, z.list_row : z.list_row + 4, :]
        for i in range(1, z.sources):
            total = total + info[group * z.sources + i, z.list_row : z.list_row + 4, :]
        ordered = total
        for i in range(1, z.sources):
            swapped = None
            for c in range(z.sources):
                part = rolled(total, (c - (c ^ i)) * z.dev_slots)
                swapped = part if c == 0 else jnp.where(lane // z.dev_slots == c, part, swapped)
            ordered = jnp.where(lax.rem(me, z.sources) == i, swapped, ordered)
        lists[group] = ordered

    keys = z.devs * z.pad
    path = lax.broadcasted_iota(jnp.int32, (z.width, LANES), 0)
    here = (
        lax.axis_index("path") * z.paths
        + (path // z.half) * z.side
        + me * z.half
        + path % z.half
    )
    total_paths = float(z.paths * z.path_devs)
    stress = STRESS * ((here.astype(F32) + 0.5) / total_paths) / float(z.months)
    key_row = lax.broadcasted_iota(jnp.int32, (keys, LANES), 0).astype(F32)
    for group in range(z.slot_groups):
        listed = lists[group].astype(jnp.int32)
        key = ((listed[2:3] ^ me) * z.pad + listed[3:4]).astype(F32)
        chooser = jnp.where(key_row == key, 1.0, 0.0).astype(BF16)
        moved = jnp.dot(source_moves[...], chooser, preferred_element_type=F32)
        level = jnp.zeros((z.width, LANES), F32)
        levels = []
        for t in range(z.months):
            level = level + (stress - moved[t * z.width : (t + 1) * z.width])
            levels.append(level)
        level = jnp.concatenate(levels, axis=0)
        high, low = pieces((0.5 * slope[0, z.live - 1]) * level, 2)
        both_pieces[group, :, 0:LANES] = high.astype(BF16)
        both_pieces[group, :, LANES:] = low.astype(BF16)
    last_base, last_rate = 0.5 * base[0, z.live - 1], 0.5 * slope[0, z.live - 1]
    roll_rate = [slope[0, k] / slope[0, z.live - 1] for k in range(z.live)]
    cure_rate = [-(slope[1, k] / slope[0, z.live - 1]) for k in range(z.live)]
    roll_base = [0.5 * base[0, k] - roll_rate[k] * last_base for k in range(z.live)]
    cure_base = [0.5 * base[1, k] - cure_rate[k] * last_base for k in range(z.live)]
    severity_rate = 3.0 / slope[0, z.live - 1]
    severity_base = -(severity_rate * last_base)
    for j in range(z.devs):
        rows = [info[j, q * z.loan_rows : (q + 1) * z.loan_rows, :] for q in range(7)]
        ltv = rows[3] + rows[4]

        def of_start(values):
            chosen = jnp.full(rows[1].shape, values[0], F32)
            for k in range(1, z.live):
                chosen = jnp.where(rows[1] == float(k), values[k], chosen)
            return chosen

        per_loan = [
            last_base + last_rate * ltv,
            rows[5] + rows[6],
            of_start([0.5**k for k in range(z.live)]),
            of_start([2.0**k for k in range(z.live)]),
        ]
        for rates in (roll_base, roll_rate, cure_base, cure_rate):
            per_loan.append(of_start(rates))
        for rates in (roll_base, roll_rate, cure_base, cure_rate):
            per_loan.append(of_start(rates[1:] + [0.0]))
        for q, value in enumerate(per_loan):
            loans[j, q * z.loan_rows : (q + 1) * z.loan_rows, :] = value
    sums[...] = jnp.zeros_like(sums)
    marks = z.dates * z.width
    slot_row = lax.broadcasted_iota(jnp.int32, (z.regions, BLOCK), 0).astype(F32)

    def row(j, b, q, values=info):
        first = q * z.loan_rows + b * z.per
        both = values[j, first : first + z.per, :]
        return jnp.concatenate([both[r : r + 1, :] for r in range(z.per)], axis=1)

    def one_hot(j, i, b, q):
        ours = jnp.where(slot_row == row(j, b, q), 1.0, 0.0).astype(BF16)
        parts = [jnp.zeros_like(ours)] * (z.sources * z.blocks)
        parts[(i % z.sources) * z.blocks + b] = ours
        return jnp.concatenate(parts, axis=0)

    def fill(first, i, b, moved):
        j = first + i
        chosen = one_hot(j, i, b, 0)
        chosen = jnp.concatenate([chosen, chosen], axis=0)
        moved[...] = jnp.dot(both_pieces[j // z.sources], chosen, preferred_element_type=F32)

    def run(first, i, b, moved):
        j = first + i
        start = row(j, b, 1)
        begins = [start == float(k) for k in range(z.live)]
        balance_rows = [row(j, b, q) for q in (5, 6)]
        own_last, balance, size, power = [row(j, b, q, loans) for q in range(4)]
        rates = [row(j, b, q, loans) for q in range(4, 12)]
        top = z.live - 1

        def step(mass, roll_offset, roll_rate, cure_offset, cure_rate, x):
            part = mass * jnp.tanh(roll_offset + roll_rate * x)
            rest = mass - part
            cured = rest * jnp.tanh(cure_offset + cure_rate * x)
            return mass + part, rest - cured, rest + cured

        state = None
        loss = jnp.zeros((z.width, BLOCK), F32)
        for t in range(z.months):
            x = moved[t * z.width : (t + 1) * z.width, :] + own_last
            ahead, keep, gain = [None] * z.live, [None] * z.live, [None] * z.live
            following = [None] * z.live
            if t == 0:
                on, stays, back = step(size, *rates[:4], x)
                ahead[top] = jnp.where(begins[top], on, 0.0)
                following = [
                    stays,
                    jnp.where(begins[top], 0.0, on),
                    jnp.where(begins[0], 0.0, power * back),
                ]
            elif t == 1:
                on, stays, back = step(state[0], *rates[:4], x)
                next_on, next_stays, next_back = step(state[1], *rates[4:], x)
                first_on, first_stays, _ = step(
                    state[2], roll_base[0], roll_rate[0], cure_base[0], cure_rate[0], x
                )
                middle = on + next_stays
                ahead[top] = jnp.where(
                    begins[top], on, jnp.where(begins[top - 1], next_on, 0.0)
                )
                for k in range(1, z.live):
                    value = jnp.where(begins[k - 2], next_on, 0.0) if k > 1 else 0.0
                    value = jnp.where(begins[k - 1], middle, value)
                    following[k] = jnp.where(begins[k], stays, value)
                following[1] = following[1] + first_on
                own = jnp.where(begins[0], stays, power * back)
                following[0] = own + (2.0 * power) * next_back + first_stays
            else:
                for k in range(z.live):
                    if t >= z.reach(k):
                        continue
                    argument = x if k == top else roll_base[k] + roll_rate[k] * x
                    part = state[k] * jnp.tanh(argument)
                    ahead[k] = state[k] + part
                    if t + 1 < z.reach(k):
                        rest = state[k] - part
                        cured = rest * jnp.tanh(cure_base[k] + cure_rate[k] * x)
                        keep[k] = rest - cured
                        gain[k] = rest + cured
                for k in range(1, z.live):
                    if t + 1 < z.reach(k):
                        following[k] = ahead[k - 1] + keep[k]
                if t + 1 < z.reach(0):
                    back = gain[top]
                    for k in range(top - 1, 0, -1):
                        back = 2.0 * back + gain[k]
                    following[0] = keep[0] + 2.0 * back
            severity = jnp.tanh(severity_base + severity_rate * x)
            scale = 0.5 * 2.0 ** (z.live - 1) * 0.25**t
            loss = loss + (0.35 * scale + (0.25 * scale) * severity) * ahead[top]
            state = following
            if t % 4 == 3:
                d = t // 4
                high, low = pieces(balance * loss, 2)
                dated[d * z.width : (d + 1) * z.width, :] = high.astype(BF16)
                dated[marks + d * z.width : marks + (d + 1) * z.width, :] = low.astype(BF16)
        money = jnp.concatenate(balance_rows + [jnp.zeros((14, BLOCK), F32)], axis=0)
        dated[2 * marks :, :] = money.astype(BF16)
        group = j // z.sources
        sums[group] = sums[group] + lax.dot_general(
            dated[...], one_hot(j, i, b, 2), (((1,), (1,)), ((), ())), preferred_element_type=F32
        )

    moved = (moved_even, moved_odd)

    unroll = min(8, z.devs)

    def source_step(step, carry):
        first = step * unroll
        order = [(first, i, b) for i in range(unroll) for b in range(z.blocks)]
        fill(*order[0], moved[0])
        for i, block in enumerate(order):
            if i + 1 < len(order):
                fill(*order[i + 1], moved[(i + 1) % 2])
            run(*block, moved[i % 2])
        return carry

    lax.fori_loop(0, z.devs // unroll, source_step, 0)

    for group in range(z.slot_groups):
        total = sums[group]
        money = total[2 * marks : 2 * marks + 1] + total[2 * marks + 1 : 2 * marks + 2]
        ratio = (total[0:marks] + total[marks : 2 * marks]) / money
        split = jnp.concatenate(pieces(ratio, 3), axis=0).astype(BF16)
        listed = lists[group]
        pool_id = listed[0:1] * 64.0 + listed[1:2]
        pool_iota = lax.broadcasted_iota(jnp.int32, (z.all_pools, LANES), 0).astype(F32)
        order = jnp.where(pool_iota == pool_id, 1.0, 0.0).astype(BF16)
        part = lax.dot_general(
            split, order, (((1,), (1,)), ((), ())), preferred_element_type=F32
        )
        part = part[0:marks] + part[marks : 2 * marks] + part[2 * marks :]
        ratios[...] = part if group == 0 else ratios[...] + part
    for c in range(z.chips):
        to = me ^ (2 * c)
        both = ratios[:, pl.ds(pl.multiple_of((to * z.pools // LANES) * LANES, LANES), LANES)]
        for d in range(z.dates):
            made = []
            for own in range(LANES // z.pools):
                mixed = None
                for h in range(z.halves):
                    first = d * z.width + h * z.half
                    part = rolled(both[first : first + z.half], (h - own) * z.pools)
                    mixed = part if mixed is None else jnp.where(lane // z.pools == h, part, mixed)
                made.append(mixed)
            odd = lax.rem(me, 2) == 1
            rows = slice(d * z.half, (d + 1) * z.half)
            outs[c][rows, :] = jnp.where(odd, made[1], made[0])
            rows = slice(z.out_rows + d * z.half, z.out_rows + (d + 1) * z.half)
            outs[c][rows, :] = jnp.where(odd, made[0], made[1])


def owned_ratio(z, near, far, j, d):
    c = j // 2
    if j % 2 == 0:
        return near[c][d * z.half : (d + 1) * z.half, :]
    return far[c * z.out_rows + d * z.half : c * z.out_rows + (d + 1) * z.half, :]


def means_kernel(z, *refs):
    near, (far, bps, out, scratch) = refs[: z.chips], refs[z.chips :]
    scratch[...] = jnp.zeros_like(scratch)
    scratch[0 : z.tranches, 0 : z.pools] = bps[...].astype(F32) / 10000.0
    rows = scratch[...]
    for h in range(1, z.halves):
        rows = rows + pltpu.roll(scratch[...], h * z.pools, 1)
    out[...] = jnp.zeros_like(out)
    for d in range(z.dates):
        ratio = jnp.concatenate(
            [owned_ratio(z, near, far, j, d) for j in range(z.devs)], axis=0
        )
        for j in range(z.tranches):
            low = rows[j : j + 1]
            height = (rows[j + 1 : j + 2] if j + 1 < z.tranches else 1.0) - low
            share = jnp.clip((ratio - low) / height, 0.0, 1.0)
            out[j * z.dates + d : j * z.dates + d + 1, :] = jnp.sum(share, axis=0, keepdims=True)


def paths_kernel(z, *refs):
    near, (far, bps, out, scratch, columns) = refs[: z.chips], refs[z.chips :]
    me = lax.axis_index("loan")
    columns[...] = jnp.zeros_like(columns)
    columns[0 : z.tranches, 0 : z.pools] = bps[...].astype(F32) / 10000.0
    attach = columns[...].T
    for j in range(z.devs):
        first = (me ^ j) * z.half
        scratch[pl.ds(first, z.half), :] = owned_ratio(z, near, far, j, z.dates - 1)
    turned = scratch[...].T
    ratio = jnp.concatenate(
        [turned[h * z.pools : (h + 1) * z.pools, 0 : z.side] for h in range(z.halves)], axis=1
    )
    for j in range(z.tranches):
        low = attach[0 : z.pools, j : j + 1]
        high = attach[0 : z.pools, j + 1 : j + 2] if j + 1 < z.tranches else 1.0
        out[j] = jnp.clip((ratio - low) / (high - low), 0.0, 1.0)


def total_kernel(z, *refs):
    terms, out = [ref[...] for ref in refs[:-1]], refs[-1]
    while len(terms) > 1:
        terms = [terms[i] + terms[i + 1] for i in range(0, len(terms), 2)]
    total = terms[0]
    wide = total
    for h in range(1, z.halves):
        wide = wide + pltpu.roll(total, LANES - h * z.pools, 1)
    wide = wide[:, 0 : z.pools] / float(z.paths * z.path_devs)
    for j in range(z.tranches):
        out[j] = wide[j * z.dates : (j + 1) * z.dates]


def grant(mib):
    return pltpu.CompilerParams(vmem_limit_bytes=mib << 20)


def exchange(z, parts, rows):
    near = [parts[0]] + [None] * (z.chips - 1)
    for c in range(z.chips - 1, 0, -1):
        near[c] = lax.ppermute(parts[c], "loan", [(i, i ^ (2 * c)) for i in range(z.devs)])
    passed = pl.pallas_call(
        functools.partial(pass_kernel, z, rows),
        out_shape=jax.ShapeDtypeStruct((z.chips * rows, LANES), parts[0].dtype),
        in_specs=[VMEM] * z.chips,
        out_specs=VMEM,
        compiler_params=grant(4),
        name="pass",
    )(*near)
    return near + [lax.ppermute(passed, "loan", [(i, i ^ 1) for i in range(z.devs)])]


def shards(
    price_moves,
    block_regions,
    region_slot,
    block_pools,
    pool_slot,
    init_state,
    balance,
    loan_to_value,
    hazard_base,
    hazard_slope,
    attach_bps,
):
    z = Sizes(price_moves, block_regions, block_pools, attach_bps, hazard_base)

    def lanes(value):
        return value.reshape(z.loan_rows, LANES)

    inputs = [
        price_moves,
        block_regions,
        block_pools,
        lanes(region_slot),
        lanes(pool_slot),
        lanes(init_state),
        lanes(balance),
        lanes(loan_to_value),
    ]
    sent = pl.pallas_call(
        functools.partial(pack_kernel, z),
        out_shape=[jax.ShapeDtypeStruct((z.sent_rows, LANES), BF16)] * z.chips,
        in_specs=[pl.BlockSpec(memory_space=pltpu.HBM)] * 8,
        out_specs=[VMEM] * z.chips,
        scratch_shapes=[pltpu.VMEM(value.shape, value.dtype) for value in inputs]
        + [
            pltpu.VMEM((z.groups, LANES, LANES), F32),
            pltpu.VMEM((z.info_rows, LANES), F32),
            pltpu.VMEM((8, LANES), F32),
            pltpu.SemaphoreType.DMA((8,)),
        ],
        compiler_params=grant(8),
        name="pack",
    )(*[pltpu.with_memory_space_constraint(value, pltpu.HBM) for value in inputs])
    parts = exchange(z, sent, z.rows)
    marks = z.dates * z.width
    moved = pltpu.VMEM((z.steps, BLOCK), F32)
    sent = pl.pallas_call(
        functools.partial(months_kernel, z),
        out_shape=[jax.ShapeDtypeStruct((2 * z.out_rows, LANES), F32)] * z.chips,
        in_specs=[VMEM] * (z.chips + 1) + [SMEM] * 2,
        out_specs=[VMEM] * z.chips,
        scratch_shapes=[
            pltpu.VMEM((z.steps, z.devs * z.pad), BF16),
            pltpu.VMEM((z.devs, z.info_rows, LANES), F32),
            pltpu.VMEM((z.devs, 12 * z.loan_rows, LANES), F32),
            pltpu.VMEM((z.slot_groups, z.steps, 2 * LANES), BF16),
            moved,
            moved,
            pltpu.VMEM((2 * marks + 16, BLOCK), BF16),
            pltpu.VMEM((z.slot_groups, 2 * marks + 16, LANES), F32),
            pltpu.VMEM((z.slot_groups, 4, LANES), F32),
            pltpu.VMEM((marks, z.all_pools), F32),
        ],
        compiler_params=grant(16),
        name="months",
    )(*parts, hazard_base, hazard_slope)
    parts = exchange(z, sent, z.out_rows)
    attach = attach_bps.T
    total_rows = -(-z.tranches * z.dates // 8) * 8
    sums = pl.pallas_call(
        functools.partial(means_kernel, z),
        out_shape=jax.ShapeDtypeStruct((total_rows, LANES), F32),
        in_specs=[VMEM] * (z.chips + 2),
        out_specs=VMEM,
        scratch_shapes=[pltpu.VMEM((8, LANES), F32)],
        compiler_params=grant(4),
        name="means",
    )(*parts, attach)
    terms = [sums] + [
        lax.ppermute(sums, "path", [(i, i ^ k) for i in range(z.path_devs)])
        for k in range(1, z.path_devs)
    ]
    path_loss = pl.pallas_call(
        functools.partial(paths_kernel, z),
        out_shape=jax.ShapeDtypeStruct((z.tranches, z.pools, z.paths), F32),
        in_specs=[VMEM] * (z.chips + 2),
        out_specs=VMEM,
        scratch_shapes=[pltpu.VMEM((z.side, LANES), F32), pltpu.VMEM((8, LANES), F32)],
        compiler_params=grant(4),
        name="paths",
    )(*parts, attach)
    expected_loss = pl.pallas_call(
        functools.partial(total_kernel, z),
        out_shape=jax.ShapeDtypeStruct((z.tranches, z.dates, z.pools), F32),
        in_specs=[VMEM] * z.path_devs,
        out_specs=VMEM,
        compiler_params=grant(4),
        name="total",
    )(*terms)
    return expected_loss, path_loss


def solution(mesh):
    in_specs = (
        P(None, "loan", "path"),
        P("loan", None),
        P("loan"),
        P("loan", None),
        P("loan"),
        P("loan"),
        P("loan"),
        P("loan"),
        P(),
        P(),
        P("loan", None),
    )
    out_specs = (P(None, None, "loan"), P(None, "loan", "path"))
    return jax.shard_map(shards, mesh=mesh, in_specs=in_specs, out_specs=out_specs, check_vma=False)
```

```python
import functools

import jax
import jax.numpy as jnp
from jax import lax
from jax.experimental import pallas as pl
from jax.experimental.pallas import tpu as pltpu
from jax.sharding import PartitionSpec as P

BLOCK = 256
LANES = 128
STRESS = 0.3
F32 = jnp.float32
BF16 = jnp.bfloat16

VMEM = pl.BlockSpec(memory_space=pltpu.VMEM)
SMEM = pl.BlockSpec(memory_space=pltpu.SMEM)


def next_pow2(value):
    return 1 << (value - 1).bit_length()


class Sizes:
    def __init__(self, price_moves, block_regions, block_pools, attach_bps, hazard_base):
        self.devs = lax.axis_size("loan")
        self.path_devs = lax.axis_size("path")
        self.chips = self.devs // 2
        self.months, self.metros, self.paths = price_moves.shape
        self.blocks, self.regions = block_regions.shape
        self.slots = block_pools.shape[1]
        self.pools, self.tranches = attach_bps.shape
        self.live = hazard_base.shape[1]
        self.dates = self.months // 4
        self.width = self.paths // self.devs
        self.halves = 2
        self.half = self.width // self.halves
        self.side = self.paths // self.halves
        self.pad = next_pow2(max(self.metros, 16))
        self.fold = LANES // self.pad
        self.groups = -(-self.months // self.fold)
        self.price_rows = self.groups * self.width
        self.per = BLOCK // LANES
        self.loan_rows = self.blocks * self.per
        self.list_row = 7 * self.loan_rows
        self.info_rows = -(-(self.list_row + 4) // 16) * 16
        self.rows = self.price_rows + self.info_rows
        self.sent_rows = self.price_rows + self.rows
        self.dev_slots = self.blocks * self.slots
        self.sources = LANES // self.dev_slots
        self.all_pools = self.pools * self.devs
        self.slot_groups = self.devs // self.sources
        self.out_rows = self.dates * self.half
        self.steps = self.months * self.width

    def reach(self, state):
        return self.months - (self.live - 1 - state)


def pieces(value, count):
    out = []
    for _ in range(count):
        piece = value.astype(BF16).astype(F32)
        out.append(piece)
        value = value - piece
    return out


def rolled(value, shift):
    shift = shift % LANES
    return value if shift == 0 else pltpu.roll(value, shift, 1)


def pack_kernel(z, *refs):
    sources, outs, scratch = refs[:8], refs[8 : 8 + z.chips], refs[8 + z.chips :]
    moves, regions, pool_lists, region, pool, init, balance, ltv = scratch[:8]
    turned, info, table, arrived = scratch[8:]
    copies = [
        pltpu.make_async_copy(source, target, arrived.at[i])
        for i, (source, target) in enumerate(zip(sources, scratch[:8]))
    ]
    for copy in copies:
        copy.start()
    for copy in copies[1:]:
        copy.wait()
    me = lax.axis_index("loan")
    info[...] = jnp.zeros_like(info)
    values = [region[...].astype(F32), init[...].astype(F32), pool[...].astype(F32)]
    values += pieces(jnp.log(ltv[...]), 2) + pieces(balance[...], 2)
    for q, value in enumerate(values):
        info[q * z.loan_rows : (q + 1) * z.loan_rows, :] = value
    lane = lax.broadcasted_iota(jnp.int32, (1, LANES), 1)
    mine = lane // z.dev_slots == lax.rem(me, z.sources)

    def spread(lists):
        table[...] = jnp.zeros_like(table)
        table[0 : z.blocks, 0 : z.slots] = lists.astype(F32)
        wide = table[...]
        row = wide[0:1, :]
        for b in range(1, z.blocks):
            row = row + pltpu.roll(wide, b * z.slots, 1)[b : b + 1, :]
        wide = row
        for c in range(1, z.sources):
            wide = wide + pltpu.roll(jnp.broadcast_to(row, (8, LANES)), c * z.dev_slots, 1)[0:1, :]
        return jnp.where(mine, wide, 0.0)

    listed = spread(pool_lists[...])
    high = jnp.floor(listed * (1.0 / 64.0))
    metro = spread(regions[...])
    owner = jnp.zeros_like(metro)
    for k in range(1, z.devs):
        owner = owner + jnp.where(metro >= float(k * z.metros), 1.0, 0.0)
    rows = [high, listed - 64.0 * high, owner, metro - owner * float(z.metros)]
    for i, row in enumerate(rows):
        info[z.list_row + i : z.list_row + i + 1, :] = row
    packed = info[...].astype(BF16)
    for c in range(z.chips):
        outs[c][2 * z.price_rows :, :] = packed
    copies[0].wait()
    for g in range(z.groups):
        parts = []
        for h in range(z.fold):
            t = h * z.groups + g
            if t < z.months:
                parts.append(moves[t].astype(F32))
            else:
                parts.append(jnp.zeros((z.metros, z.paths), F32))
            if z.pad > z.metros:
                parts.append(jnp.zeros((z.pad - z.metros, z.paths), F32))
        turned[g] = jnp.concatenate(parts, axis=0).T
    for c in range(z.chips):
        for other in range(2):
            to = me ^ (2 * c + other)
            for g in range(z.groups):
                both = [
                    turned[g, pl.ds(h * z.side + to * z.half, z.half), :] for h in range(z.halves)
                ]
                first = other * z.price_rows + g * z.width
                outs[c][first : first + z.width, :] = jnp.concatenate(both, axis=0).astype(BF16)


def pass_kernel(z, rows, *refs):
    parts, out = refs[:-1], refs[-1]
    for c, part in enumerate(parts):
        out[c * rows : (c + 1) * rows, :] = part[part.shape[0] - rows :, :]


def months_kernel(z, *refs):
    near, (far, base, slope), outs = (
        refs[: z.chips],
        refs[z.chips : z.chips + 3],
        refs[z.chips + 3 : 2 * z.chips + 3],
    )
    (
        source_moves,
        info,
        loans,
        both_pieces,
        moved_even,
        moved_odd,
        dated,
        sums,
        lists,
        ratios,
    ) = refs[2 * z.chips + 3 :]
    me = lax.axis_index("loan")
    lane = lax.broadcasted_iota(jnp.int32, (1, LANES), 1)

    def prices_of(j):
        c = j // 2
        if j % 2 == 0:
            return near[c][0 : z.price_rows, :]
        return far[c * z.rows : c * z.rows + z.price_rows, :]

    for j in range(z.devs // z.fold):
        parts = []
        for i in range(z.fold):
            parts.append(prices_of(j * z.fold + i).astype(F32))
        for h in range(z.fold):
            mixed = None
            count = min(z.groups, z.months - h * z.groups) * z.width
            if count <= 0:
                continue
            for i in range(z.fold):
                part = rolled(parts[i], (i - h) * z.pad)
                mixed = part if mixed is None else jnp.where(lane // z.pad == i, part, mixed)
            first = h * z.price_rows
            source_moves[first : first + count, j * LANES : (j + 1) * LANES] = mixed[
                0:count
            ].astype(BF16)
    for j in range(z.devs):
        c = j // 2
        if j % 2 == 0:
            part = near[c][2 * z.price_rows :, :]
        else:
            part = far[c * z.rows + z.price_rows : (c + 1) * z.rows, :]
        info[j] = part.astype(F32)
    for group in range(z.slot_groups):
        total = info[group * z.sources, z.list_row : z.list_row + 4, :]
        for i in range(1, z.sources):
            total = total + info[group * z.sources + i, z.list_row : z.list_row + 4, :]
        ordered = total
        for i in range(1, z.sources):
            swapped = None
            for c in range(z.sources):
                part = rolled(total, (c - (c ^ i)) * z.dev_slots)
                swapped = part if c == 0 else jnp.where(lane // z.dev_slots == c, part, swapped)
            ordered = jnp.where(lax.rem(me, z.sources) == i, swapped, ordered)
        lists[group] = ordered

    keys = z.devs * z.pad
    path = lax.broadcasted_iota(jnp.int32, (z.width, LANES), 0)
    here = (
        lax.axis_index("path") * z.paths
        + (path // z.half) * z.side
        + me * z.half
        + path % z.half
    )
    total_paths = float(z.paths * z.path_devs)
    stress = STRESS * ((here.astype(F32) + 0.5) / total_paths) / float(z.months)
    key_row = lax.broadcasted_iota(jnp.int32, (keys, LANES), 0).astype(F32)
    for group in range(z.slot_groups):
        listed = lists[group].astype(jnp.int32)
        key = ((listed[2:3] ^ me) * z.pad + listed[3:4]).astype(F32)
        chooser = jnp.where(key_row == key, 1.0, 0.0).astype(BF16)
        moved = jnp.dot(source_moves[...], chooser, preferred_element_type=F32)
        level = jnp.zeros((z.width, LANES), F32)
        levels = []
        for t in range(z.months):
            level = level + (stress - moved[t * z.width : (t + 1) * z.width])
            levels.append(level)
        level = jnp.concatenate(levels, axis=0)
        high, low = pieces((0.5 * slope[0, z.live - 1]) * level, 2)
        both_pieces[group, :, 0:LANES] = high.astype(BF16)
        both_pieces[group, :, LANES:] = low.astype(BF16)
    last_base, last_rate = 0.5 * base[0, z.live - 1], 0.5 * slope[0, z.live - 1]
    roll_rate = [slope[0, k] / slope[0, z.live - 1] for k in range(z.live)]
    cure_rate = [-(slope[1, k] / slope[0, z.live - 1]) for k in range(z.live)]
    roll_base = [0.5 * base[0, k] - roll_rate[k] * last_base for k in range(z.live)]
    cure_base = [0.5 * base[1, k] - cure_rate[k] * last_base for k in range(z.live)]
    severity_rate = 3.0 / slope[0, z.live - 1]
    severity_base = -(severity_rate * last_base)
    for j in range(z.devs):
        rows = [info[j, q * z.loan_rows : (q + 1) * z.loan_rows, :] for q in range(7)]
        ltv = rows[3] + rows[4]

        def of_start(values):
            chosen = jnp.full(rows[1].shape, values[0], F32)
            for k in range(1, z.live):
                chosen = jnp.where(rows[1] == float(k), values[k], chosen)
            return chosen

        per_loan = [
            last_base + last_rate * ltv,
            rows[5] + rows[6],
            of_start([0.5**k for k in range(z.live)]),
            of_start([2.0**k for k in range(z.live)]),
        ]
        for rates in (roll_base, roll_rate, cure_base, cure_rate):
            per_loan.append(of_start(rates))
        for rates in (roll_base, roll_rate, cure_base, cure_rate):
            per_loan.append(of_start(rates[1:] + [0.0]))
        for q, value in enumerate(per_loan):
            loans[j, q * z.loan_rows : (q + 1) * z.loan_rows, :] = value
    sums[...] = jnp.zeros_like(sums)
    marks = z.dates * z.width
    slot_row = lax.broadcasted_iota(jnp.int32, (z.regions, BLOCK), 0).astype(F32)

    def row(j, b, q, values=info):
        first = q * z.loan_rows + b * z.per
        both = values[j, first : first + z.per, :]
        return jnp.concatenate([both[r : r + 1, :] for r in range(z.per)], axis=1)

    def one_hot(j, i, b, q):
        ours = jnp.where(slot_row == row(j, b, q), 1.0, 0.0).astype(BF16)
        parts = [jnp.zeros_like(ours)] * (z.sources * z.blocks)
        parts[(i % z.sources) * z.blocks + b] = ours
        return jnp.concatenate(parts, axis=0)

    def fill(first, i, b, moved):
        j = first + i
        chosen = one_hot(j, i, b, 0)
        chosen = jnp.concatenate([chosen, chosen], axis=0)
        moved[...] = jnp.dot(both_pieces[j // z.sources], chosen, preferred_element_type=F32)

    def run(first, i, b, moved):
        j = first + i
        start = row(j, b, 1)
        begins = [start == float(k) for k in range(z.live)]
        balance_rows = [row(j, b, q) for q in (5, 6)]
        own_last, balance, size, power = [row(j, b, q, loans) for q in range(4)]
        rates = [row(j, b, q, loans) for q in range(4, 12)]
        top = z.live - 1

        def step(mass, roll_offset, roll_rate, cure_offset, cure_rate, x):
            part = mass * jnp.tanh(roll_offset + roll_rate * x)
            rest = mass - part
            cured = rest * jnp.tanh(cure_offset + cure_rate * x)
            return mass + part, rest - cured, rest + cured

        state = None
        loss = jnp.zeros((z.width, BLOCK), F32)
        for t in range(z.months):
            x = moved[t * z.width : (t + 1) * z.width, :] + own_last
            ahead, keep, gain = [None] * z.live, [None] * z.live, [None] * z.live
            following = [None] * z.live
            if t == 0:
                on, stays, back = step(size, *rates[:4], x)
                ahead[top] = jnp.where(begins[top], on, 0.0)
                following = [
                    stays,
                    jnp.where(begins[top], 0.0, on),
                    jnp.where(begins[0], 0.0, power * back),
                ]
            elif t == 1:
                on, stays, back = step(state[0], *rates[:4], x)
                next_on, next_stays, next_back = step(state[1], *rates[4:], x)
                first_on, first_stays, _ = step(
                    state[2], roll_base[0], roll_rate[0], cure_base[0], cure_rate[0], x
                )
                middle = on + next_stays
                ahead[top] = jnp.where(
                    begins[top], on, jnp.where(begins[top - 1], next_on, 0.0)
                )
                for k in range(1, z.live):
                    value = jnp.where(begins[k - 2], next_on, 0.0) if k > 1 else 0.0
                    value = jnp.where(begins[k - 1], middle, value)
                    following[k] = jnp.where(begins[k], stays, value)
                following[1] = following[1] + first_on
                own = jnp.where(begins[0], stays, power * back)
                following[0] = own + (2.0 * power) * next_back + first_stays
            else:
                for k in range(z.live):
                    if t >= z.reach(k):
                        continue
                    argument = x if k == top else roll_base[k] + roll_rate[k] * x
                    part = state[k] * jnp.tanh(argument)
                    ahead[k] = state[k] + part
                    if t + 1 < z.reach(k):
                        rest = state[k] - part
                        cured = rest * jnp.tanh(cure_base[k] + cure_rate[k] * x)
                        keep[k] = rest - cured
                        gain[k] = rest + cured
                for k in range(1, z.live):
                    if t + 1 < z.reach(k):
                        following[k] = ahead[k - 1] + keep[k]
                if t + 1 < z.reach(0):
                    back = gain[top]
                    for k in range(top - 1, 0, -1):
                        back = 2.0 * back + gain[k]
                    following[0] = keep[0] + 2.0 * back
            severity = jnp.tanh(severity_base + severity_rate * x)
            scale = 0.5 * 2.0 ** (z.live - 1) * 0.25**t
            loss = loss + (0.35 * scale + (0.25 * scale) * severity) * ahead[top]
            state = following
            if t % 4 == 3:
                d = t // 4
                high, low = pieces(balance * loss, 2)
                dated[d * z.width : (d + 1) * z.width, :] = high.astype(BF16)
                dated[marks + d * z.width : marks + (d + 1) * z.width, :] = low.astype(BF16)
        money = jnp.concatenate(balance_rows + [jnp.zeros((14, BLOCK), F32)], axis=0)
        dated[2 * marks :, :] = money.astype(BF16)
        group = j // z.sources
        sums[group] = sums[group] + lax.dot_general(
            dated[...], one_hot(j, i, b, 2), (((1,), (1,)), ((), ())), preferred_element_type=F32
        )

    moved = (moved_even, moved_odd)

    unroll = min(8, z.devs)

    def source_step(step, carry):
        first = step * unroll
        order = [(first, i, b) for i in range(unroll) for b in range(z.blocks)]
        fill(*order[0], moved[0])
        for i, block in enumerate(order):
            if i + 1 < len(order):
                fill(*order[i + 1], moved[(i + 1) % 2])
            run(*block, moved[i % 2])
        return carry

    lax.fori_loop(0, z.devs // unroll, source_step, 0)

    for group in range(z.slot_groups):
        total = sums[group]
        money = total[2 * marks : 2 * marks + 1] + total[2 * marks + 1 : 2 * marks + 2]
        ratio = (total[0:marks] + total[marks : 2 * marks]) / money
        split = jnp.concatenate(pieces(ratio, 3), axis=0).astype(BF16)
        listed = lists[group]
        pool_id = listed[0:1] * 64.0 + listed[1:2]
        pool_iota = lax.broadcasted_iota(jnp.int32, (z.all_pools, LANES), 0).astype(F32)
        order = jnp.where(pool_iota == pool_id, 1.0, 0.0).astype(BF16)
        part = lax.dot_general(
            split, order, (((1,), (1,)), ((), ())), preferred_element_type=F32
        )
        part = part[0:marks] + part[marks : 2 * marks] + part[2 * marks :]
        ratios[...] = part if group == 0 else ratios[...] + part
    for c in range(z.chips):
        to = me ^ (2 * c)
        both = ratios[:, pl.ds(pl.multiple_of((to * z.pools // LANES) * LANES, LANES), LANES)]
        for d in range(z.dates):
            made = []
            for own in range(LANES // z.pools):
                mixed = None
                for h in range(z.halves):
                    first = d * z.width + h * z.half
                    part = rolled(both[first : first + z.half], (h - own) * z.pools)
                    mixed = part if mixed is None else jnp.where(lane // z.pools == h, part, mixed)
                made.append(mixed)
            odd = lax.rem(me, 2) == 1
            rows = slice(d * z.half, (d + 1) * z.half)
            outs[c][rows, :] = jnp.where(odd, made[1], made[0])
            rows = slice(z.out_rows + d * z.half, z.out_rows + (d + 1) * z.half)
            outs[c][rows, :] = jnp.where(odd, made[0], made[1])


def owned_ratio(z, near, far, j, d):
    c = j // 2
    if j % 2 == 0:
        return near[c][d * z.half : (d + 1) * z.half, :]
    return far[c * z.out_rows + d * z.half : c * z.out_rows + (d + 1) * z.half, :]


def means_kernel(z, *refs):
    near, (far, bps, out, scratch) = refs[: z.chips], refs[z.chips :]
    scratch[...] = jnp.zeros_like(scratch)
    scratch[0 : z.tranches, 0 : z.pools] = bps[...].astype(F32) / 10000.0
    rows = scratch[...]
    for h in range(1, z.halves):
        rows = rows + pltpu.roll(scratch[...], h * z.pools, 1)
    out[...] = jnp.zeros_like(out)
    for d in range(z.dates):
        ratio = jnp.concatenate(
            [owned_ratio(z, near, far, j, d) for j in range(z.devs)], axis=0
        )
        for j in range(z.tranches):
            low = rows[j : j + 1]
            height = (rows[j + 1 : j + 2] if j + 1 < z.tranches else 1.0) - low
            share = jnp.clip((ratio - low) / height, 0.0, 1.0)
            out[j * z.dates + d : j * z.dates + d + 1, :] = jnp.sum(share, axis=0, keepdims=True)


def paths_kernel(z, *refs):
    near, (far, bps, out, scratch, columns) = refs[: z.chips], refs[z.chips :]
    me = lax.axis_index("loan")
    columns[...] = jnp.zeros_like(columns)
    columns[0 : z.tranches, 0 : z.pools] = bps[...].astype(F32) / 10000.0
    attach = columns[...].T
    for j in range(z.devs):
        first = (me ^ j) * z.half
        scratch[pl.ds(first, z.half), :] = owned_ratio(z, near, far, j, z.dates - 1)
    turned = scratch[...].T
    ratio = jnp.concatenate(
        [turned[h * z.pools : (h + 1) * z.pools, 0 : z.side] for h in range(z.halves)], axis=1
    )
    for j in range(z.tranches):
        low = attach[0 : z.pools, j : j + 1]
        high = attach[0 : z.pools, j + 1 : j + 2] if j + 1 < z.tranches else 1.0
        out[j] = jnp.clip((ratio - low) / (high - low), 0.0, 1.0)


def total_kernel(z, *refs):
    terms, out = [ref[...] for ref in refs[:-1]], refs[-1]
    while len(terms) > 1:
        terms = [terms[i] + terms[i + 1] for i in range(0, len(terms), 2)]
    total = terms[0]
    wide = total
    for h in range(1, z.halves):
        wide = wide + pltpu.roll(total, LANES - h * z.pools, 1)
    wide = wide[:, 0 : z.pools] / float(z.paths * z.path_devs)
    for j in range(z.tranches):
        out[j] = wide[j * z.dates : (j + 1) * z.dates]


def grant(mib):
    return pltpu.CompilerParams(vmem_limit_bytes=mib << 20)


def exchange(z, parts, rows):
    near = [parts[0]] + [None] * (z.chips - 1)
    for c in range(z.chips - 1, 0, -1):
        near[c] = lax.ppermute(parts[c], "loan", [(i, i ^ (2 * c)) for i in range(z.devs)])
    passed = pl.pallas_call(
        functools.partial(pass_kernel, z, rows),
        out_shape=jax.ShapeDtypeStruct((z.chips * rows, LANES), parts[0].dtype),
        in_specs=[VMEM] * z.chips,
        out_specs=VMEM,
        compiler_params=grant(4),
        name="pass",
    )(*near)
    return near + [lax.ppermute(passed, "loan", [(i, i ^ 1) for i in range(z.devs)])]


def shards(
    price_moves,
    block_regions,
    region_slot,
    block_pools,
    pool_slot,
    init_state,
    balance,
    loan_to_value,
    hazard_base,
    hazard_slope,
    attach_bps,
):
    z = Sizes(price_moves, block_regions, block_pools, attach_bps, hazard_base)

    def lanes(value):
        return value.reshape(z.loan_rows, LANES)

    inputs = [
        price_moves,
        block_regions,
        block_pools,
        lanes(region_slot),
        lanes(pool_slot),
        lanes(init_state),
        lanes(balance),
        lanes(loan_to_value),
    ]
    sent = pl.pallas_call(
        functools.partial(pack_kernel, z),
        out_shape=[jax.ShapeDtypeStruct((z.sent_rows, LANES), BF16)] * z.chips,
        in_specs=[pl.BlockSpec(memory_space=pltpu.HBM)] * 8,
        out_specs=[VMEM] * z.chips,
        scratch_shapes=[pltpu.VMEM(value.shape, value.dtype) for value in inputs]
        + [
            pltpu.VMEM((z.groups, LANES, LANES), F32),
            pltpu.VMEM((z.info_rows, LANES), F32),
            pltpu.VMEM((8, LANES), F32),
            pltpu.SemaphoreType.DMA((8,)),
        ],
        compiler_params=grant(8),
        name="pack",
    )(*[pltpu.with_memory_space_constraint(value, pltpu.HBM) for value in inputs])
    parts = exchange(z, sent, z.rows)
    marks = z.dates * z.width
    moved = pltpu.VMEM((z.steps, BLOCK), F32)
    sent = pl.pallas_call(
        functools.partial(months_kernel, z),
        out_shape=[jax.ShapeDtypeStruct((2 * z.out_rows, LANES), F32)] * z.chips,
        in_specs=[VMEM] * (z.chips + 1) + [SMEM] * 2,
        out_specs=[VMEM] * z.chips,
        scratch_shapes=[
            pltpu.VMEM((z.steps, z.devs * z.pad), BF16),
            pltpu.VMEM((z.devs, z.info_rows, LANES), F32),
            pltpu.VMEM((z.devs, 12 * z.loan_rows, LANES), F32),
            pltpu.VMEM((z.slot_groups, z.steps, 2 * LANES), BF16),
            moved,
            moved,
            pltpu.VMEM((2 * marks + 16, BLOCK), BF16),
            pltpu.VMEM((z.slot_groups, 2 * marks + 16, LANES), F32),
            pltpu.VMEM((z.slot_groups, 4, LANES), F32),
            pltpu.VMEM((marks, z.all_pools), F32),
        ],
        compiler_params=pltpu.CompilerParams(vmem_limit_bytes=16 << 20),
        name="months",
    )(*parts, hazard_base, hazard_slope)
    parts = exchange(z, sent, z.out_rows)
    attach = attach_bps.T
    total_rows = -(-z.tranches * z.dates // 8) * 8
    sums = pl.pallas_call(
        functools.partial(means_kernel, z),
        out_shape=jax.ShapeDtypeStruct((total_rows, LANES), F32),
        in_specs=[VMEM] * (z.chips + 2),
        out_specs=VMEM,
        scratch_shapes=[pltpu.VMEM((8, LANES), F32)],
        compiler_params=grant(4),
        name="means",
    )(*parts, attach)
    terms = [sums] + [
        lax.ppermute(sums, "path", [(i, i ^ k) for i in range(z.path_devs)])
        for k in range(1, z.path_devs)
    ]
    path_loss = pl.pallas_call(
        functools.partial(paths_kernel, z),
        out_shape=jax.ShapeDtypeStruct((z.tranches, z.pools, z.paths), F32),
        in_specs=[VMEM] * (z.chips + 2),
        out_specs=VMEM,
        scratch_shapes=[pltpu.VMEM((z.side, LANES), F32), pltpu.VMEM((8, LANES), F32)],
        compiler_params=grant(4),
        name="paths",
    )(*parts, attach)
    expected_loss = pl.pallas_call(
        functools.partial(total_kernel, z),
        out_shape=jax.ShapeDtypeStruct((z.tranches, z.dates, z.pools), F32),
        in_specs=[VMEM] * z.path_devs,
        out_specs=VMEM,
        compiler_params=grant(4),
        name="total",
    )(*terms)
    return expected_loss, path_loss


def solution(mesh):
    in_specs = (
        P(None, "loan", "path"),
        P("loan", None),
        P("loan"),
        P("loan", None),
        P("loan"),
        P("loan"),
        P("loan"),
        P("loan"),
        P(),
        P(),
        P("loan", None),
    )
    out_specs = (P(None, None, "loan"), P(None, "loan", "path"))
    return jax.shard_map(shards, mesh=mesh, in_specs=in_specs, out_specs=out_specs, check_vma=False)
```

```python
import functools

import jax
import jax.numpy as jnp
from jax import lax
from jax.experimental import pallas as pl
from jax.experimental.pallas import tpu as pltpu
from jax.sharding import PartitionSpec as P

BLOCK = 256
LANES = 128
STRESS = 0.3
F32 = jnp.float32
BF16 = jnp.bfloat16

VMEM = pl.BlockSpec(memory_space=pltpu.VMEM)
SMEM = pl.BlockSpec(memory_space=pltpu.SMEM)


def next_pow2(value):
    return 1 << (value - 1).bit_length()


class Sizes:
    def __init__(self, price_moves, block_regions, block_pools, attach_bps, hazard_base):
        self.devs = lax.axis_size("loan")
        self.path_devs = lax.axis_size("path")
        self.chips = self.devs // 2
        self.months, self.metros, self.paths = price_moves.shape
        self.blocks, self.regions = block_regions.shape
        self.slots = block_pools.shape[1]
        self.pools, self.tranches = attach_bps.shape
        self.live = hazard_base.shape[1]
        self.dates = self.months // 4
        self.width = self.paths // self.devs
        self.halves = 2
        self.half = self.width // self.halves
        self.side = self.paths // self.halves
        self.pad = next_pow2(max(self.metros, 16))
        self.fold = LANES // self.pad
        self.groups = -(-self.months // self.fold)
        self.price_rows = self.groups * self.width
        self.per = BLOCK // LANES
        self.loan_rows = self.blocks * self.per
        self.list_row = 7 * self.loan_rows
        self.info_rows = -(-(self.list_row + 4) // 16) * 16
        self.rows = self.price_rows + self.info_rows
        self.sent_rows = self.price_rows + self.rows
        self.dev_slots = self.blocks * self.slots
        self.sources = LANES // self.dev_slots
        self.all_pools = self.pools * self.devs
        self.slot_groups = self.devs // self.sources
        self.out_rows = self.dates * self.half
        self.steps = self.months * self.width

    def reach(self, state):
        return self.months - (self.live - 1 - state)


def pieces(value, count):
    out = []
    for _ in range(count):
        piece = value.astype(BF16).astype(F32)
        out.append(piece)
        value = value - piece
    return out


def rolled(value, shift):
    shift = shift % LANES
    return value if shift == 0 else pltpu.roll(value, shift, 1)


def pack_kernel(z, *refs):
    sources, outs, scratch = refs[:8], refs[8 : 8 + z.chips], refs[8 + z.chips :]
    moves, regions, pool_lists, region, pool, init, balance, ltv = scratch[:8]
    turned, info, table, arrived = scratch[8:]
    copies = [
        pltpu.make_async_copy(source, target, arrived.at[i])
        for i, (source, target) in enumerate(zip(sources, scratch[:8]))
    ]
    for copy in copies:
        copy.start()
    for copy in copies[1:]:
        copy.wait()
    me = lax.axis_index("loan")
    info[...] = jnp.zeros_like(info)
    values = [region[...].astype(F32), init[...].astype(F32), pool[...].astype(F32)]
    values += pieces(jnp.log(ltv[...]), 2) + pieces(balance[...], 2)
    for q, value in enumerate(values):
        info[q * z.loan_rows : (q + 1) * z.loan_rows, :] = value
    lane = lax.broadcasted_iota(jnp.int32, (1, LANES), 1)
    mine = lane // z.dev_slots == lax.rem(me, z.sources)

    def spread(lists):
        table[...] = jnp.zeros_like(table)
        table[0 : z.blocks, 0 : z.slots] = lists.astype(F32)
        wide = table[...]
        row = wide[0:1, :]
        for b in range(1, z.blocks):
            row = row + pltpu.roll(wide, b * z.slots, 1)[b : b + 1, :]
        wide = row
        for c in range(1, z.sources):
            wide = wide + pltpu.roll(jnp.broadcast_to(row, (8, LANES)), c * z.dev_slots, 1)[0:1, :]
        return jnp.where(mine, wide, 0.0)

    listed = spread(pool_lists[...])
    high = jnp.floor(listed * (1.0 / 64.0))
    metro = spread(regions[...])
    owner = jnp.zeros_like(metro)
    for k in range(1, z.devs):
        owner = owner + jnp.where(metro >= float(k * z.metros), 1.0, 0.0)
    rows = [high, listed - 64.0 * high, owner, metro - owner * float(z.metros)]
    for i, row in enumerate(rows):
        info[z.list_row + i : z.list_row + i + 1, :] = row
    packed = info[...].astype(BF16)
    for c in range(z.chips):
        outs[c][2 * z.price_rows :, :] = packed
    copies[0].wait()
    for g in range(z.groups):
        parts = []
        for h in range(z.fold):
            t = h * z.groups + g
            if t < z.months:
                parts.append(moves[t].astype(F32))
            else:
                parts.append(jnp.zeros((z.metros, z.paths), F32))
            if z.pad > z.metros:
                parts.append(jnp.zeros((z.pad - z.metros, z.paths), F32))
        turned[g] = jnp.concatenate(parts, axis=0).T
    for c in range(z.chips):
        for other in range(2):
            to = me ^ (2 * c + other)
            for g in range(z.groups):
                both = [
                    turned[g, pl.ds(h * z.side + to * z.half, z.half), :] for h in range(z.halves)
                ]
                first = other * z.price_rows + g * z.width
                outs[c][first : first + z.width, :] = jnp.concatenate(both, axis=0).astype(BF16)


def pass_kernel(z, rows, *refs):
    parts, out = refs[:-1], refs[-1]
    for c, part in enumerate(parts):
        out[c * rows : (c + 1) * rows, :] = part[part.shape[0] - rows :, :]


def months_kernel(z, *refs):
    near, (far, base, slope), outs = (
        refs[: z.chips],
        refs[z.chips : z.chips + 3],
        refs[z.chips + 3 : 2 * z.chips + 3],
    )
    (
        source_moves,
        info,
        loans,
        both_pieces,
        moved_even,
        moved_odd,
        dated,
        sums,
        lists,
        ratios,
    ) = refs[2 * z.chips + 3 :]
    me = lax.axis_index("loan")
    lane = lax.broadcasted_iota(jnp.int32, (1, LANES), 1)

    def prices_of(j):
        c = j // 2
        if j % 2 == 0:
            return near[c][0 : z.price_rows, :]
        return far[c * z.rows : c * z.rows + z.price_rows, :]

    for j in range(z.devs // z.fold):
        parts = []
        for i in range(z.fold):
            parts.append(prices_of(j * z.fold + i).astype(F32))
        for h in range(z.fold):
            mixed = None
            count = min(z.groups, z.months - h * z.groups) * z.width
            if count <= 0:
                continue
            for i in range(z.fold):
                part = rolled(parts[i], (i - h) * z.pad)
                mixed = part if mixed is None else jnp.where(lane // z.pad == i, part, mixed)
            first = h * z.price_rows
            source_moves[first : first + count, j * LANES : (j + 1) * LANES] = mixed[
                0:count
            ].astype(BF16)
    for j in range(z.devs):
        c = j // 2
        if j % 2 == 0:
            part = near[c][2 * z.price_rows :, :]
        else:
            part = far[c * z.rows + z.price_rows : (c + 1) * z.rows, :]
        info[j] = part.astype(F32)
    for group in range(z.slot_groups):
        total = info[group * z.sources, z.list_row : z.list_row + 4, :]
        for i in range(1, z.sources):
            total = total + info[group * z.sources + i, z.list_row : z.list_row + 4, :]
        ordered = total
        for i in range(1, z.sources):
            swapped = None
            for c in range(z.sources):
                part = rolled(total, (c - (c ^ i)) * z.dev_slots)
                swapped = part if c == 0 else jnp.where(lane // z.dev_slots == c, part, swapped)
            ordered = jnp.where(lax.rem(me, z.sources) == i, swapped, ordered)
        lists[group] = ordered

    keys = z.devs * z.pad
    path = lax.broadcasted_iota(jnp.int32, (z.width, LANES), 0)
    here = (
        lax.axis_index("path") * z.paths
        + (path // z.half) * z.side
        + me * z.half
        + path % z.half
    )
    total_paths = float(z.paths * z.path_devs)
    stress = STRESS * ((here.astype(F32) + 0.5) / total_paths) / float(z.months)
    key_row = lax.broadcasted_iota(jnp.int32, (keys, LANES), 0).astype(F32)
    for pair in range(0, z.slot_groups, 2):
        choosers = []
        for group in (pair, pair + 1):
            listed = lists[group].astype(jnp.int32)
            key = ((listed[2:3] ^ me) * z.pad + listed[3:4]).astype(F32)
            choosers.append(jnp.where(key_row == key, 1.0, 0.0).astype(BF16))
        both = jnp.dot(
            source_moves[...], jnp.concatenate(choosers, axis=1), preferred_element_type=F32
        )
        for group in (pair, pair + 1):
            moved_now = both[:, (group - pair) * LANES : (group - pair + 1) * LANES]
            level = jnp.zeros((z.width, LANES), F32)
            levels = []
            for t in range(z.months):
                level = level + (stress - moved_now[t * z.width : (t + 1) * z.width])
                levels.append(level)
            level = jnp.concatenate(levels, axis=0)
            high, low = pieces((0.5 * slope[0, z.live - 1]) * level, 2)
            both_pieces[group, :, 0:LANES] = high.astype(BF16)
            both_pieces[group, :, LANES:] = low.astype(BF16)
    last_base, last_rate = 0.5 * base[0, z.live - 1], 0.5 * slope[0, z.live - 1]
    roll_rate = [slope[0, k] / slope[0, z.live - 1] for k in range(z.live)]
    cure_rate = [-(slope[1, k] / slope[0, z.live - 1]) for k in range(z.live)]
    roll_base = [0.5 * base[0, k] - roll_rate[k] * last_base for k in range(z.live)]
    cure_base = [0.5 * base[1, k] - cure_rate[k] * last_base for k in range(z.live)]
    severity_rate = 3.0 / slope[0, z.live - 1]
    severity_base = -(severity_rate * last_base)
    for j in range(z.devs):
        rows = [info[j, q * z.loan_rows : (q + 1) * z.loan_rows, :] for q in range(7)]
        ltv = rows[3] + rows[4]

        def of_start(values):
            chosen = jnp.full(rows[1].shape, values[0], F32)
            for k in range(1, z.live):
                chosen = jnp.where(rows[1] == float(k), values[k], chosen)
            return chosen

        per_loan = [
            last_base + last_rate * ltv,
            rows[5] + rows[6],
            of_start([0.5**k for k in range(z.live)]),
            of_start([2.0**k for k in range(z.live)]),
        ]
        for rates in (roll_base, roll_rate, cure_base, cure_rate):
            per_loan.append(of_start(rates))
        for rates in (roll_base, roll_rate, cure_base, cure_rate):
            per_loan.append(of_start(rates[1:] + [0.0]))
        for q, value in enumerate(per_loan):
            loans[j, q * z.loan_rows : (q + 1) * z.loan_rows, :] = value
    sums[...] = jnp.zeros_like(sums)
    marks = z.dates * z.width
    slot_row = lax.broadcasted_iota(jnp.int32, (z.regions, BLOCK), 0).astype(F32)

    def row(j, b, q, values=info):
        first = q * z.loan_rows + b * z.per
        both = values[j, first : first + z.per, :]
        return jnp.concatenate([both[r : r + 1, :] for r in range(z.per)], axis=1)

    def one_hot(j, i, b, q):
        ours = jnp.where(slot_row == row(j, b, q), 1.0, 0.0).astype(BF16)
        parts = [jnp.zeros_like(ours)] * (z.sources * z.blocks)
        parts[(i % z.sources) * z.blocks + b] = ours
        return jnp.concatenate(parts, axis=0)

    def fill(first, i, b, moved):
        j = first + i
        chosen = one_hot(j, i, b, 0)
        chosen = jnp.concatenate([chosen, chosen], axis=0)
        moved[...] = jnp.dot(both_pieces[j // z.sources], chosen, preferred_element_type=F32)

    def run(first, i, b, moved):
        j = first + i
        start = row(j, b, 1)
        begins = [start == float(k) for k in range(z.live)]
        balance_rows = [row(j, b, q) for q in (5, 6)]
        own_last, balance, size, power = [row(j, b, q, loans) for q in range(4)]
        rates = [row(j, b, q, loans) for q in range(4, 12)]
        top = z.live - 1

        def step(mass, roll_offset, roll_rate, cure_offset, cure_rate, x):
            part = mass * jnp.tanh(roll_offset + roll_rate * x)
            rest = mass - part
            cured = rest * jnp.tanh(cure_offset + cure_rate * x)
            return mass + part, rest - cured, rest + cured

        state = None
        loss = jnp.zeros((z.width, BLOCK), F32)
        for t in range(z.months):
            x = moved[t * z.width : (t + 1) * z.width, :] + own_last
            ahead, keep, gain = [None] * z.live, [None] * z.live, [None] * z.live
            following = [None] * z.live
            if t == 0:
                on, stays, back = step(size, *rates[:4], x)
                ahead[top] = jnp.where(begins[top], on, 0.0)
                following = [
                    stays,
                    jnp.where(begins[top], 0.0, on),
                    jnp.where(begins[0], 0.0, power * back),
                ]
            elif t == 1:
                on, stays, back = step(state[0], *rates[:4], x)
                next_on, next_stays, next_back = step(state[1], *rates[4:], x)
                first_on, first_stays, _ = step(
                    state[2], roll_base[0], roll_rate[0], cure_base[0], cure_rate[0], x
                )
                middle = on + next_stays
                ahead[top] = jnp.where(
                    begins[top], on, jnp.where(begins[top - 1], next_on, 0.0)
                )
                for k in range(1, z.live):
                    value = jnp.where(begins[k - 2], next_on, 0.0) if k > 1 else 0.0
                    value = jnp.where(begins[k - 1], middle, value)
                    following[k] = jnp.where(begins[k], stays, value)
                following[1] = following[1] + first_on
                own = jnp.where(begins[0], stays, power * back)
                following[0] = own + (2.0 * power) * next_back + first_stays
            else:
                for k in range(z.live):
                    if t >= z.reach(k):
                        continue
                    argument = x if k == top else roll_base[k] + roll_rate[k] * x
                    part = state[k] * jnp.tanh(argument)
                    ahead[k] = state[k] + part
                    if t + 1 < z.reach(k):
                        rest = state[k] - part
                        cured = rest * jnp.tanh(cure_base[k] + cure_rate[k] * x)
                        keep[k] = rest - cured
                        gain[k] = rest + cured
                for k in range(1, z.live):
                    if t + 1 < z.reach(k):
                        following[k] = ahead[k - 1] + keep[k]
                if t + 1 < z.reach(0):
                    back = gain[top]
                    for k in range(top - 1, 0, -1):
                        back = 2.0 * back + gain[k]
                    following[0] = keep[0] + 2.0 * back
            severity = jnp.tanh(severity_base + severity_rate * x)
            scale = 0.5 * 2.0 ** (z.live - 1) * 0.25**t
            loss = loss + (0.35 * scale + (0.25 * scale) * severity) * ahead[top]
            state = following
            if t % 4 == 3:
                d = t // 4
                high, low = pieces(balance * loss, 2)
                dated[d * z.width : (d + 1) * z.width, :] = high.astype(BF16)
                dated[marks + d * z.width : marks + (d + 1) * z.width, :] = low.astype(BF16)
        money = jnp.concatenate(balance_rows + [jnp.zeros((14, BLOCK), F32)], axis=0)
        dated[2 * marks :, :] = money.astype(BF16)
        group = j // z.sources
        sums[group] = sums[group] + lax.dot_general(
            dated[...], one_hot(j, i, b, 2), (((1,), (1,)), ((), ())), preferred_element_type=F32
        )

    moved = (moved_even, moved_odd)

    unroll = min(8, z.devs)

    def source_step(step, carry):
        first = step * unroll
        order = [(first, i, b) for i in range(unroll) for b in range(z.blocks)]
        fill(*order[0], moved[0])
        for i, block in enumerate(order):
            if i + 1 < len(order):
                fill(*order[i + 1], moved[(i + 1) % 2])
            run(*block, moved[i % 2])
        return carry

    lax.fori_loop(0, z.devs // unroll, source_step, 0)

    for group in range(z.slot_groups):
        total = sums[group]
        money = total[2 * marks : 2 * marks + 1] + total[2 * marks + 1 : 2 * marks + 2]
        ratio = (total[0:marks] + total[marks : 2 * marks]) / money
        split = jnp.concatenate(pieces(ratio, 3), axis=0).astype(BF16)
        listed = lists[group]
        pool_id = listed[0:1] * 64.0 + listed[1:2]
        pool_iota = lax.broadcasted_iota(jnp.int32, (z.all_pools, LANES), 0).astype(F32)
        order = jnp.where(pool_iota == pool_id, 1.0, 0.0).astype(BF16)
        part = lax.dot_general(
            split, order, (((1,), (1,)), ((), ())), preferred_element_type=F32
        )
        part = part[0:marks] + part[marks : 2 * marks] + part[2 * marks :]
        ratios[...] = part if group == 0 else ratios[...] + part
    for c in range(z.chips):
        to = me ^ (2 * c)
        both = ratios[:, pl.ds(pl.multiple_of((to * z.pools // LANES) * LANES, LANES), LANES)]
        for d in range(z.dates):
            made = []
            for own in range(LANES // z.pools):
                mixed = None
                for h in range(z.halves):
                    first = d * z.width + h * z.half
                    part = rolled(both[first : first + z.half], (h - own) * z.pools)
                    mixed = part if mixed is None else jnp.where(lane // z.pools == h, part, mixed)
                made.append(mixed)
            odd = lax.rem(me, 2) == 1
            rows = slice(d * z.half, (d + 1) * z.half)
            outs[c][rows, :] = jnp.where(odd, made[1], made[0])
            rows = slice(z.out_rows + d * z.half, z.out_rows + (d + 1) * z.half)
            outs[c][rows, :] = jnp.where(odd, made[0], made[1])


def owned_ratio(z, near, far, j, d):
    c = j // 2
    if j % 2 == 0:
        return near[c][d * z.half : (d + 1) * z.half, :]
    return far[c * z.out_rows + d * z.half : c * z.out_rows + (d + 1) * z.half, :]


def means_kernel(z, *refs):
    near, (far, bps, out, scratch) = refs[: z.chips], refs[z.chips :]
    scratch[...] = jnp.zeros_like(scratch)
    scratch[0 : z.tranches, 0 : z.pools] = bps[...].astype(F32) / 10000.0
    rows = scratch[...]
    for h in range(1, z.halves):
        rows = rows + pltpu.roll(scratch[...], h * z.pools, 1)
    out[...] = jnp.zeros_like(out)
    for d in range(z.dates):
        ratio = jnp.concatenate(
            [owned_ratio(z, near, far, j, d) for j in range(z.devs)], axis=0
        )
        for j in range(z.tranches):
            low = rows[j : j + 1]
            height = (rows[j + 1 : j + 2] if j + 1 < z.tranches else 1.0) - low
            share = jnp.clip((ratio - low) / height, 0.0, 1.0)
            out[j * z.dates + d : j * z.dates + d + 1, :] = jnp.sum(share, axis=0, keepdims=True)


def paths_kernel(z, *refs):
    near, (far, bps, out, scratch, columns) = refs[: z.chips], refs[z.chips :]
    me = lax.axis_index("loan")
    columns[...] = jnp.zeros_like(columns)
    columns[0 : z.tranches, 0 : z.pools] = bps[...].astype(F32) / 10000.0
    attach = columns[...].T
    for j in range(z.devs):
        first = (me ^ j) * z.half
        scratch[pl.ds(first, z.half), :] = owned_ratio(z, near, far, j, z.dates - 1)
    turned = scratch[...].T
    ratio = jnp.concatenate(
        [turned[h * z.pools : (h + 1) * z.pools, 0 : z.side] for h in range(z.halves)], axis=1
    )
    for j in range(z.tranches):
        low = attach[0 : z.pools, j : j + 1]
        high = attach[0 : z.pools, j + 1 : j + 2] if j + 1 < z.tranches else 1.0
        out[j] = jnp.clip((ratio - low) / (high - low), 0.0, 1.0)


def total_kernel(z, *refs):
    terms, out = [ref[...] for ref in refs[:-1]], refs[-1]
    while len(terms) > 1:
        terms = [terms[i] + terms[i + 1] for i in range(0, len(terms), 2)]
    total = terms[0]
    wide = total
    for h in range(1, z.halves):
        wide = wide + pltpu.roll(total, LANES - h * z.pools, 1)
    wide = wide[:, 0 : z.pools] / float(z.paths * z.path_devs)
    for j in range(z.tranches):
        out[j] = wide[j * z.dates : (j + 1) * z.dates]


def grant(mib):
    return pltpu.CompilerParams(vmem_limit_bytes=mib << 20)


def exchange(z, parts, rows):
    near = [parts[0]] + [None] * (z.chips - 1)
    for c in range(z.chips - 1, 0, -1):
        near[c] = lax.ppermute(parts[c], "loan", [(i, i ^ (2 * c)) for i in range(z.devs)])
    passed = pl.pallas_call(
        functools.partial(pass_kernel, z, rows),
        out_shape=jax.ShapeDtypeStruct((z.chips * rows, LANES), parts[0].dtype),
        in_specs=[VMEM] * z.chips,
        out_specs=VMEM,
        compiler_params=grant(4),
        name="pass",
    )(*near)
    return near + [lax.ppermute(passed, "loan", [(i, i ^ 1) for i in range(z.devs)])]


def shards(
    price_moves,
    block_regions,
    region_slot,
    block_pools,
    pool_slot,
    init_state,
    balance,
    loan_to_value,
    hazard_base,
    hazard_slope,
    attach_bps,
):
    z = Sizes(price_moves, block_regions, block_pools, attach_bps, hazard_base)

    def lanes(value):
        return value.reshape(z.loan_rows, LANES)

    inputs = [
        price_moves,
        block_regions,
        block_pools,
        lanes(region_slot),
        lanes(pool_slot),
        lanes(init_state),
        lanes(balance),
        lanes(loan_to_value),
    ]
    sent = pl.pallas_call(
        functools.partial(pack_kernel, z),
        out_shape=[jax.ShapeDtypeStruct((z.sent_rows, LANES), BF16)] * z.chips,
        in_specs=[pl.BlockSpec(memory_space=pltpu.HBM)] * 8,
        out_specs=[VMEM] * z.chips,
        scratch_shapes=[pltpu.VMEM(value.shape, value.dtype) for value in inputs]
        + [
            pltpu.VMEM((z.groups, LANES, LANES), F32),
            pltpu.VMEM((z.info_rows, LANES), F32),
            pltpu.VMEM((8, LANES), F32),
            pltpu.SemaphoreType.DMA((8,)),
        ],
        compiler_params=grant(8),
        name="pack",
    )(*[pltpu.with_memory_space_constraint(value, pltpu.HBM) for value in inputs])
    parts = exchange(z, sent, z.rows)
    marks = z.dates * z.width
    moved = pltpu.VMEM((z.steps, BLOCK), F32)
    sent = pl.pallas_call(
        functools.partial(months_kernel, z),
        out_shape=[jax.ShapeDtypeStruct((2 * z.out_rows, LANES), F32)] * z.chips,
        in_specs=[VMEM] * (z.chips + 1) + [SMEM] * 2,
        out_specs=[VMEM] * z.chips,
        scratch_shapes=[
            pltpu.VMEM((z.steps, z.devs * z.pad), BF16),
            pltpu.VMEM((z.devs, z.info_rows, LANES), F32),
            pltpu.VMEM((z.devs, 12 * z.loan_rows, LANES), F32),
            pltpu.VMEM((z.slot_groups, z.steps, 2 * LANES), BF16),
            moved,
            moved,
            pltpu.VMEM((2 * marks + 16, BLOCK), BF16),
            pltpu.VMEM((z.slot_groups, 2 * marks + 16, LANES), F32),
            pltpu.VMEM((z.slot_groups, 4, LANES), F32),
            pltpu.VMEM((marks, z.all_pools), F32),
        ],
        compiler_params=pltpu.CompilerParams(
            vmem_limit_bytes=16 << 20
        ),
        name="months",
    )(*parts, hazard_base, hazard_slope)
    parts = exchange(z, sent, z.out_rows)
    attach = attach_bps.T
    total_rows = -(-z.tranches * z.dates // 8) * 8
    sums = pl.pallas_call(
        functools.partial(means_kernel, z),
        out_shape=jax.ShapeDtypeStruct((total_rows, LANES), F32),
        in_specs=[VMEM] * (z.chips + 2),
        out_specs=VMEM,
        scratch_shapes=[pltpu.VMEM((8, LANES), F32)],
        compiler_params=grant(4),
        name="means",
    )(*parts, attach)
    terms = [sums] + [
        lax.ppermute(sums, "path", [(i, i ^ k) for i in range(z.path_devs)])
        for k in range(1, z.path_devs)
    ]
    path_loss = pl.pallas_call(
        functools.partial(paths_kernel, z),
        out_shape=jax.ShapeDtypeStruct((z.tranches, z.pools, z.paths), F32),
        in_specs=[VMEM] * (z.chips + 2),
        out_specs=VMEM,
        scratch_shapes=[pltpu.VMEM((z.side, LANES), F32), pltpu.VMEM((8, LANES), F32)],
        compiler_params=grant(4),
        name="paths",
    )(*parts, attach)
    expected_loss = pl.pallas_call(
        functools.partial(total_kernel, z),
        out_shape=jax.ShapeDtypeStruct((z.tranches, z.dates, z.pools), F32),
        in_specs=[VMEM] * z.path_devs,
        out_specs=VMEM,
        compiler_params=grant(4),
        name="total",
    )(*terms)
    return expected_loss, path_loss


def solution(mesh):
    in_specs = (
        P(None, "loan", "path"),
        P("loan", None),
        P("loan"),
        P("loan", None),
        P("loan"),
        P("loan"),
        P("loan"),
        P("loan"),
        P(),
        P(),
        P("loan", None),
    )
    out_specs = (P(None, None, "loan"), P(None, "loan", "path"))
    return jax.shard_map(shards, mesh=mesh, in_specs=in_specs, out_specs=out_specs, check_vma=False)
```
